512 devices in a mesh: ctx: 128 (over y, z, x_lo), fft: 4 (over x_hi, core).
Axes of the slice: x: 4 (x_hi: 2, x_lo: 2; x = x_hi * 2 + x_lo), y: 8, z: 8, core: 2. Of those that a mesh axis runs over, the one named last changes fastest.
Arguments:
- streams: bfloat16 [3, 16384, 2048], P(None, 'ctx', 'fft'), may hold values from -6 to 6
- taps: float32 [3, 7, 2048], P(None, None, 'fft'), may hold values from -2 to 2
- filters: bfloat16 [16384, 2048], P('ctx', 'fft')
- cotangent: bfloat16 [16384, 2048], P('ctx', 'fft')
Outputs:
- gated: bfloat16 [16384, 2048], P('ctx', 'fft')
- stream_grad: bfloat16 [3, 16384, 2048], P(None, 'ctx', 'fft')
- filter_grad: bfloat16 [16384, 2048], P('ctx', 'fft')
- tap_grad: float32 [3, 7, 2048], P(None, None, 'fft')
The draws below stay inside these ranges and needn't reach their ends.
All inputs are finite; a program needn't handle non-finite values.
Results may differ from the reference program's by a relative error of at most 0.012.
Values may be sent and summed in bfloat16 or wider, within the bound.
A program may use at most 64 MiB of HBM per device.

```python
import math
import jax
import jax.numpy as jnp
from jax import lax

CH = 2048
TAPS = 7
SEQ = 16384


def draw_filters(key, part):
    scale_factor = SEQ ** (-0.5)
    values = jnp.clip(jax.random.normal(key, (SEQ, CH), jnp.float32), -4.0, 4.0) * scale_factor
    return values.astype(jnp.bfloat16)


def draw_cotangent(key, part):
    position = jnp.arange(SEQ, dtype=jnp.float32)[:, None] / (SEQ - 1)
    noise_part = jnp.clip(jax.random.normal(key, (SEQ, CH), jnp.float32), -4.0, 4.0)
    growth = 1.0 + 2.0 * position
    return (noise_part * growth).astype(jnp.bfloat16)


def block_scale(stream_key, shape, cuts, smallest, high):
    factor_of = 1.0
    for dim, blocks in cuts:
        steps = jax.random.uniform(jax.random.fold_in(jax.random.fold_in(stream_key, 6), dim), (blocks,), jnp.float32, smallest / len(cuts), high / len(cuts))
        factor_of = factor_of * jnp.repeat(jnp.exp(steps), shape[dim] // blocks).reshape((-1,) + (1,) * (len(shape) - 1 - dim))
    return factor_of


def centred(key, extent, width, bound, cuts=(), held_as=jnp.bfloat16):
    drawn = width * jax.random.normal(key, extent, jnp.float32)
    if cuts:
        drawn = drawn * block_scale(key, extent, cuts, -0.22, 0.18)
    return jnp.clip(drawn, -bound, bound).astype(held_as)


def setup_inputs(seed: int = 0) -> dict:
    streams_of = jax.random.split(jax.random.key(seed), 5)
    streams = centred(streams_of[0], (3, SEQ, CH), 1.0, 6.0, ((1, 128), (2, 4)))
    taps = centred(streams_of[1], (3, TAPS, CH), TAPS ** -0.5, 2.0, ((2, 4),), jnp.float32)
    filters = draw_filters(jax.random.fold_in(streams_of[4], 71), 0)
    cotangent = draw_cotangent(jax.random.fold_in(streams_of[4], 71), 0)
    return dict(streams=streams, taps=taps, filters=filters, cotangent=cotangent)


def short_conv(streams, taps):
    tap_reach = taps.shape[1] - 1
    widened = jnp.pad(streams.astype(jnp.float32), ((0, 0), (tap_reach, 0), (0, 0)))
    running = jnp.zeros((3, SEQ, CH), jnp.float32)
    for offset in range(tap_reach + 1):
        running = running + taps[:, offset, None, :].astype(jnp.float32) * widened[:, tap_reach - offset:tap_reach - offset + SEQ, :]
    return (running, widened)

def spectrum(values):
    return jnp.fft.rfft(values.astype(jnp.float32), n=2 * SEQ, axis=0)

def inverse_spectrum(spec):
    return jnp.fft.irfft(spec, n=2 * SEQ, axis=0)[:SEQ]

def reference(streams, taps, filters, cotangent):
    convolved, widened = short_conv(streams, taps)
    query_side = convolved[0]
    key_side = convolved[1]
    value_side = convolved[2]
    product = (key_side * value_side).astype(jnp.bfloat16)
    product_spec = spectrum(product)
    filter_spec = spectrum(filters)
    mixed = inverse_spectrum(product_spec * filter_spec).astype(jnp.bfloat16)
    mixed_wide = mixed.astype(jnp.float32)
    gated = (query_side * mixed_wide).astype(jnp.bfloat16)
    upstream = cotangent.astype(jnp.float32)
    mixed_grad = (upstream * query_side).astype(jnp.bfloat16)
    query_grad = upstream * mixed_wide
    grad_spec = spectrum(mixed_grad)
    product_grad = inverse_spectrum(jnp.conj(filter_spec) * grad_spec).astype(jnp.bfloat16)
    scale_factor = 1.0 / math.sqrt(SEQ)
    filter_grad = (inverse_spectrum(jnp.conj(product_spec) * grad_spec) * scale_factor).astype(jnp.bfloat16)
    product_wide = product_grad.astype(jnp.float32)
    conv_grad = jnp.stack([query_grad, product_wide * value_side, product_wide * key_side])
    tap_reach = taps.shape[1] - 1
    extended_grad = jnp.pad(conv_grad, ((0, 0), (0, tap_reach), (0, 0)))
    running = jnp.zeros((3, SEQ, CH), jnp.float32)
    for offset in range(tap_reach + 1):
        running = running + taps[:, offset, None, :].astype(jnp.float32) * extended_grad[:, offset:offset + SEQ, :]
    stream_grad = running.astype(jnp.bfloat16)
    tap_terms = jnp.stack([lax.optimization_barrier(jnp.sum(conv_grad * widened[:, tap_reach - offset:tap_reach - offset + SEQ, :], axis=1)) for offset in range(tap_reach + 1)], axis=1)
    tap_grad = tap_terms * scale_factor
    return (gated, stream_grad, filter_grad, tap_grad)
```

```python
import functools
import math

import jax
import jax.numpy as jnp
import numpy as np
from jax import lax
from jax.experimental import pallas as pl
from jax.experimental.pallas import tpu as pltpu
from jax.sharding import PartitionSpec as P

MESH = pl.DeviceIdType.MESH
VMEM = pltpu.VMEM


def exchange_kernel(count, shared, *refs):
    number = len(shared)
    sources, targets, (send_sem, recv_sem, own_sem) = refs[:number], refs[number : 2 * number], refs[2 * number :]
    me = lax.axis_index("ctx")
    barrier = pltpu.get_barrier_semaphore()

    def greet(step, carry):
        peer = lax.rem(me + step, count)
        pl.semaphore_signal(barrier, inc=1, device_id={"ctx": peer}, device_id_type=MESH)
        return carry

    lax.fori_loop(1, count, greet, 0)
    own = [
        pltpu.make_async_copy(source if whole else source.at[me], target.at[me], own_sem.at[i])
        for i, (source, target, whole) in enumerate(zip(sources, targets, shared))
    ]
    for copy in own:
        copy.start()
    pl.semaphore_wait(barrier, count - 1)

    def send(step, carry):
        peer = lax.rem(me + step, count)
        for i, (source, target, whole) in enumerate(zip(sources, targets, shared)):
            pltpu.make_async_remote_copy(
                source if whole else source.at[peer],
                target.at[me],
                send_sem.at[i],
                recv_sem.at[i],
                device_id={"ctx": peer},
                device_id_type=MESH,
            ).start()
        return carry

    lax.fori_loop(1, count, send, 0)
    for copy in own:
        copy.wait()
    for i, target in enumerate(targets):
        others = target.at[pl.ds(0, count - 1)]
        whole = pltpu.make_async_remote_copy(
            others, others, send_sem.at[i], recv_sem.at[i], device_id={"ctx": me}, device_id_type=MESH
        )
        whole.wait_send()
        whole.wait_recv()


def exchange(arrays, shared, collective_id):
    count = lax.axis_size("ctx")
    outs = [
        jax.ShapeDtypeStruct((count,) + tuple(a.shape) if whole else a.shape, a.dtype)
        for a, whole in zip(arrays, shared)
    ]
    number = len(arrays)
    return pl.pallas_call(
        functools.partial(exchange_kernel, count, shared),
        out_shape=outs,
        in_specs=[pl.BlockSpec(memory_space=VMEM)] * number,
        out_specs=[pl.BlockSpec(memory_space=VMEM)] * number,
        scratch_shapes=[pltpu.SemaphoreType.DMA((number,))] * 3,
        compiler_params=pltpu.CompilerParams(collective_id=collective_id, has_side_effects=True),
    )(*arrays)


def tables(a_size, b_size):
    k1, a, b, k2 = (np.arange(n, dtype=np.int64) for n in (a_size, a_size, b_size, b_size))
    first = (4 * k1[:, None] + 1) * a[None, :] % (4 * a_size) / (4.0 * a_size)
    twist = (4 * k1[:, None] + 1) * b[None, :] % (4 * a_size * b_size) / (4.0 * a_size * b_size)
    second = b[:, None] * k2[None, :] % b_size / float(b_size)
    return [np.exp(-2j * np.pi * x).astype(np.complex64) for x in (first, twist, second)]


def owner_math(streams, filters, cotangent, taps):
    _, chans, a_size, b_size = streams.shape
    total = a_size * b_size
    reach = taps.shape[1] - 1
    first, twist, second = tables(a_size, b_size)
    dot = functools.partial(jnp.einsum, precision=lax.Precision.HIGHEST, preferred_element_type=jnp.float32)
    e1 = np.concatenate([first.real, first.imag], 0)
    e2 = np.block([[second.real, second.imag], [-second.imag, second.real]])
    back = np.concatenate([first.real.T, first.imag.T], 1) / total
    twr, twi = jnp.asarray(twist.real), jnp.asarray(twist.imag)

    def forward(x):
        y = dot("ka,cab->ckb", jnp.asarray(e1), x.astype(jnp.float32))
        re, im = y[:, :a_size], y[:, a_size:]
        turned = jnp.concatenate([re * twr - im * twi, re * twi + im * twr], -1)
        z = dot("ckb,bq->ckq", turned, jnp.asarray(e2))
        return z[..., :b_size], z[..., b_size:]

    def inverse(re, im):
        u = dot("ckq,bq->ckb", jnp.concatenate([re, im], -1), jnp.asarray(e2))
        ur, ui = u[..., :b_size], u[..., b_size:]
        turned = jnp.concatenate([ur * twr + ui * twi, ui * twr - ur * twi], 1)
        return dot("ak,ckb->cab", jnp.asarray(back), turned)

    flat = streams.astype(jnp.float32).reshape(3, chans, total)
    wide = jnp.pad(flat, ((0, 0), (0, 0), (reach, 0)))
    shifts = [wide[..., reach - j : reach - j + total] for j in range(reach + 1)]
    query, key, value = sum(taps[:, j, :, None] * shifts[j] for j in range(reach + 1))
    upstream = cotangent.astype(jnp.float32).reshape(chans, total)
    grid = (chans, a_size, b_size)
    pr, pi = forward((key * value).astype(jnp.bfloat16).reshape(grid))
    fr, fi = forward(filters)
    gr, gi = forward((upstream * query).astype(jnp.bfloat16).reshape(grid))
    mixed = inverse(pr * fr - pi * fi, pr * fi + pi * fr).astype(jnp.bfloat16).astype(jnp.float32).reshape(chans, total)
    pgrad = inverse(fr * gr + fi * gi, fr * gi - fi * gr).astype(jnp.bfloat16).astype(jnp.float32).reshape(chans, total)
    scale = 1.0 / math.sqrt(total)
    fgrad = (inverse(pr * gr + pi * gi, pr * gi - pi * gr) * scale).astype(jnp.bfloat16)
    gated = (query * mixed).astype(jnp.bfloat16).reshape(grid)
    cgrad = jnp.stack([upstream * mixed, pgrad * value, pgrad * key])
    after = jnp.pad(cgrad, ((0, 0), (0, 0), (0, reach)))
    sgrad = sum(taps[:, j, :, None] * after[..., j : j + total] for j in range(reach + 1)).astype(jnp.bfloat16)
    tgrad = jnp.stack([jnp.sum(cgrad * shifts[j], axis=-1) for j in range(reach + 1)], 1) * scale
    return gated, sgrad.reshape((3,) + grid), fgrad, tgrad


def local(streams, taps, filters, cotangent):
    rows, width = filters.shape
    owners = lax.axis_size("ctx")
    chans = width // owners
    everything = jnp.concatenate([streams, filters[None], cotangent[None]], 0)
    outgoing = everything.swapaxes(1, 2).reshape(5, owners, chans, rows).swapaxes(0, 1)
    (arrived,) = exchange([outgoing], (False,), 0)
    grid = arrived.transpose(1, 2, 0, 3)
    mine = lax.dynamic_slice_in_dim(taps, lax.axis_index("ctx") * chans, chans, 2)
    gated, sgrad, fgrad, tgrad = owner_math(grid[:3], grid[3], grid[4], mine)
    results = jnp.concatenate([gated[None], sgrad, fgrad[None]], 0).transpose(2, 0, 1, 3)
    small = jnp.pad(tgrad.reshape(1, -1), ((0, 0), (0, 128 - tgrad.size)))
    back, tall = exchange([results, small], (False, True), 1)
    back = back.swapaxes(0, 1).reshape(5, width, rows).swapaxes(1, 2)
    tap_grad = tall[:, 0, : tgrad.size].reshape((owners,) + tgrad.shape).transpose(1, 2, 0, 3).reshape(taps.shape)
    return back[0], back[1:4], back[4], tap_grad


def solution(mesh):
    in_specs = (P(None, "ctx", "fft"), P(None, None, "fft"), P("ctx", "fft"), P("ctx", "fft"))
    out_specs = (P("ctx", "fft"), P(None, "ctx", "fft"), P("ctx", "fft"), P(None, None, "fft"))
    return jax.shard_map(local, mesh=mesh, in_specs=in_specs, out_specs=out_specs, check_vma=False)
```

```python
import math

import jax
import jax.numpy as jnp
import numpy as np
from jax import lax
from jax.experimental import pallas as pl
from jax.experimental.pallas import tpu as pltpu
from jax.sharding import PartitionSpec as P

MESH = pl.DeviceIdType.MESH
VMEM = pltpu.VMEM
F32 = jnp.float32
BF16 = jnp.bfloat16
CHANS = 4
TILE = 128
ENTRIES = 24


def halves(table):
    high = table.astype(BF16)
    return high, (table - high.astype(np.float64)).astype(BF16)


def make_tables(a_size, b_size):
    k1, a, b, k2 = (np.arange(n, dtype=np.int64) for n in (a_size, a_size, b_size, b_size))
    first = (4 * k1[:, None] + 1) * a[None, :] % (4 * a_size) / (4.0 * a_size)
    twist = (4 * k1[:, None] + 1) * b[None, :] % (4 * a_size * b_size) / (4.0 * a_size * b_size)
    second = b[:, None] * k2[None, :] % b_size / float(b_size)
    first, twist, second = (np.exp(-2j * np.pi * x) for x in (first, twist, second))
    e1 = np.concatenate([first.real, first.imag], 0)
    e2 = np.block([[second.real, second.imag], [-second.imag, second.real]])
    back = np.concatenate([first.real.T, first.imag.T], 1) / (a_size * b_size)
    e1 = np.concatenate(halves(e1), 1)
    e2, e2t, back = (np.stack(halves(x)) for x in (e2, e2.T, back))
    twist = np.stack([np.tile(x, (1, 2)) for x in (twist.real, twist.imag)]).astype(np.float32)
    return e1, e2, e2t, back, twist


def dot(a, b):
    return jnp.dot(a, b, preferred_element_type=F32)


def split(x):
    high = x.astype(BF16)
    return high, (x - high.astype(F32)).astype(BF16)


def block_kernel(
    streams_hbm, filters_hbm, cot_hbm, taps_hbm, e1_hbm, e2_hbm, e2t_hbm, back_hbm, tw_hbm, taps_s,
    gated_ref, sgrad_ref, fgrad_ref, tgrad_ref,
    st, fl, ct, taps, e1, e2, e2t, back, tw,
    snd1, snd2, rcv1, rcv2, grid, shifts, qkv, spec, rows, ret_snd, ret_rcv,
    sums, small, tall, halo, ext, local_qkv, cgrad,
    in_sem, own_sem, send_sem, recv_sem,
):
    count = rcv1.shape[0]
    reach = taps.shape[1] - 1
    scale = 1.0 / math.sqrt(count * TILE)
    me = lax.axis_index("ctx")
    barrier = pltpu.get_barrier_semaphore()

    def remote(source, target, sem, peer):
        return pltpu.make_async_remote_copy(
            source, target, send_sem.at[sem], recv_sem.at[sem], device_id={"ctx": peer}, device_id_type=MESH
        )

    def greet(step, carry):
        pl.semaphore_signal(
            barrier, inc=1, device_id={"ctx": lax.rem(me + step, count)}, device_id_type=MESH
        )
        return carry

    loads = [
        pltpu.make_async_copy(source, target, in_sem.at[i])
        for i, (source, target) in enumerate(
            (
                (streams_hbm, st), (filters_hbm, fl), (cot_hbm, ct), (taps_hbm, taps), (e1_hbm, e1),
                (e2_hbm, e2), (e2t_hbm, e2t), (back_hbm, back), (tw_hbm, tw),
            )
        )
    ]
    for load in loads:
        load.start()
    lax.fori_loop(1, count, greet, 0)

    def turn_out(source, target):
        for q in range(source.shape[1] // TILE):
            tile = source[:, q * TILE : (q + 1) * TILE].astype(F32).T
            target[pl.ds(q * TILE // CHANS, TILE // CHANS)] = tile.astype(BF16).reshape(-1, CHANS, TILE)

    loads[0].wait()
    turn_out(st.at[1], snd1.at[:, 0])
    turn_out(st.at[2], snd1.at[:, 1])
    loads[1].wait()
    turn_out(fl, snd1.at[:, 2])
    turn_out(st.at[0], snd2.at[:, 0])
    loads[2].wait()
    turn_out(ct, snd2.at[:, 1])
    for load in loads[3:]:
        load.wait()

    def scatter(source, target, sem):
        own = pltpu.make_async_copy(source.at[me], target.at[me], own_sem.at[sem])
        own.start()

        def send(step, carry):
            peer = lax.rem(me + step, count)
            remote(source.at[peer], target.at[me], sem, peer).start()
            return carry

        lax.fori_loop(1, count, send, 0)
        return own

    def others(source, target, sem):
        return remote(source.at[pl.ds(0, count - 1)], target.at[pl.ds(0, count - 1)], sem, me)

    pl.semaphore_wait(barrier, count - 1)
    own1 = scatter(snd1, rcv1, 0)
    halo_out = remote(st.at[:, pl.ds(TILE - 16, 16)], halo, 6, lax.rem(me + 1, count))
    halo_in = remote(st.at[:, pl.ds(TILE - 16, 16)], halo, 6, me)

    @pl.when(me < count - 1)
    def _():
        halo_out.start()

    own2 = scatter(snd2, rcv2, 1)

    sums[...] = jnp.zeros_like(sums)
    grid[:, pl.ds(0, 8), :] = jnp.zeros((5, 8, TILE), F32)
    ext[:, pl.ds(8, TILE), :] = st[...].astype(F32)

    @pl.when(me > 0)
    def _():
        halo_in.wait_recv()
        ext[:, pl.ds(0, 8), :] = halo[...].astype(F32)[:, 8:, :]

    @pl.when(me == 0)
    def _():
        ext[:, pl.ds(0, 8), :] = jnp.zeros((3, 8, ext.shape[2]), F32)

    for i in range(3):
        for q in range(ext.shape[2] // TILE):
            lanes = pl.ds(q * TILE, TILE)
            total = None
            for j in range(reach + 1):
                term = taps[i, pl.ds(j, 1), lanes] * ext[i, pl.ds(8 - j, TILE), lanes]
                total = term if total is None else total + term
            local_qkv[i, :, lanes] = total

    lane = lax.broadcasted_iota(jnp.int32, (TILE, TILE), 1)

    def unpack(source, index):
        grid[index, pl.ds(8, count * CHANS), :] = source[...].astype(F32).reshape(count * CHANS, TILE)

    def plane(index, c):
        return grid[index, pl.ds(8 + c, count, stride=CHANS), :]

    def convolve(index, c):
        here = plane(index, c)
        before = grid[index, pl.ds(8 - CHANS + c, count, stride=CHANS), :]
        channel = CHANS * me + c
        total = taps_s[index, 0, channel] * here
        for j in range(1, reach + 1):
            moved = pltpu.roll(jnp.where(lane >= TILE - j, before, here), j, 1)
            shifts[index, c, j] = moved
            total = total + taps_s[index, j, channel] * moved
        qkv[index, c] = total
        return total

    def forward(planes, index, h):
        x = jnp.concatenate(planes, 1)
        y = dot(e1[...], jnp.concatenate([x, x], 0))
        re, im = y[:count], y[count:]
        twr, twi = tw[0], tw[1]
        tre, tim = re * twr - im * twi, re * twi + im * twr
        turned = jnp.concatenate(
            [jnp.concatenate([v[:, n * TILE : (n + 1) * TILE] for v in (tre, tim)], 1) for n in range(2)], 0
        )
        high, low = split(turned)
        spec[index, h] = dot(high, e2[0]) + dot(low, e2[0]) + dot(high, e2[1])

    def spectrum(index, h):
        return spec[index, h, :, pl.ds(0, TILE)], spec[index, h, :, pl.ds(TILE, TILE)]

    def inverse(re, im):
        high, low = split(jnp.concatenate([re, im], 1))
        u = dot(high, e2t[0]) + dot(low, e2t[0]) + dot(high, e2t[1])
        ur = jnp.concatenate([u[:count, :TILE], u[count:, :TILE]], 1)
        ui = jnp.concatenate([u[:count, TILE:], u[count:, TILE:]], 1)
        twr, twi = tw[0], tw[1]
        high, low = split(jnp.concatenate([ur * twr + ui * twi, ui * twr - ur * twi], 0))
        return dot(back[0], high) + dot(back[1], high) + dot(back[0], low)

    def put_rows(h, y):
        for n in range(2):
            rows[pl.ds(2 * h + n, count, stride=CHANS), :] = y[:, n * TILE : (n + 1) * TILE]

    def pack(which):
        ret_snd[which] = rows[...].astype(BF16).reshape(count, CHANS, TILE)

    def tap_sums(index, c, grad):
        for j in range(reach + 1):
            moved = plane(index, c) if j == 0 else shifts[index, c, j]
            part = jnp.sum((grad * moved).reshape(count // 8, 8, TILE), 0)
            sums[c * ENTRIES + index * (reach + 1) + j] = part

    own1.wait()
    others(snd1, rcv1, 0).wait_recv()
    for k, index in enumerate((1, 2, 3)):
        unpack(rcv1.at[:, k], index)
    for h in range(2):
        products, kernels = [], []
        for c in (2 * h, 2 * h + 1):
            products.append((convolve(1, c) * convolve(2, c)).astype(BF16))
            kernels.append(plane(3, c).astype(BF16))
        forward(products, 0, h)
        forward(kernels, 1, h)
        pr, pi = spectrum(0, h)
        fr, fi = spectrum(1, h)
        put_rows(h, inverse(pr * fr - pi * fi, pr * fi + pi * fr))
    pack(0)
    own3 = scatter(ret_snd.at[0], ret_rcv.at[0], 2)

    own2.wait()
    others(snd2, rcv2, 1).wait_recv()
    unpack(rcv2.at[:, 0], 0)
    unpack(rcv2.at[:, 1], 4)
    for h in range(2):
        grads = []
        for c in (2 * h, 2 * h + 1):
            upstream = plane(4, c)
            grads.append((upstream * convolve(0, c)).astype(BF16))
            mixed = rows[pl.ds(c, count, stride=CHANS), :].astype(BF16).astype(F32)
            tap_sums(0, c, upstream * mixed)
        forward(grads, 2, h)
    for h in range(2):
        fr, fi = spectrum(1, h)
        gr, gi = spectrum(2, h)
        y = inverse(fr * gr + fi * gi, fr * gi - fi * gr)
        put_rows(h, y)
    pack(1)
    own4 = scatter(ret_snd.at[1], ret_rcv.at[1], 3)
    for c in range(CHANS):
        pgrad = rows[pl.ds(c, count, stride=CHANS), :].astype(BF16).astype(F32)
        tap_sums(1, c, pgrad * qkv[2, c])
        tap_sums(2, c, pgrad * qkv[1, c])
    for h in range(2):
        pr, pi = spectrum(0, h)
        gr, gi = spectrum(2, h)
        put_rows(h, inverse(pr * gr + pi * gi, pr * gi - pi * gr) * scale)
    pack(2)
    own5 = scatter(ret_snd.at[2], ret_rcv.at[2], 4)
    entries = jnp.sum(sums[...], 1)
    row = lax.dot_general(
        jnp.ones((8, TILE), F32), entries, (((1,), (1,)), ((), ())),
        precision=lax.Precision.HIGHEST, preferred_element_type=F32,
    )
    small[...] = row[0:1] * scale
    own6 = pltpu.make_async_copy(small, tall.at[me], own_sem.at[5])
    own6.start()

    def share(step, carry):
        remote(small, tall.at[me], 5, lax.rem(me + step, count)).start()
        return carry

    lax.fori_loop(1, count, share, 0)

    def turn_back(source, q):
        tile = source[pl.ds(q * TILE // CHANS, TILE // CHANS)].astype(F32).reshape(TILE, TILE)
        return tile.T

    strips = [pl.ds(q * TILE, TILE) for q in range(ext.shape[2] // TILE)]
    own3.wait()
    others(ret_snd.at[0], ret_rcv.at[0], 2).wait_recv()
    for q, lanes in enumerate(strips):
        mixed = turn_back(ret_rcv.at[0], q)
        gated_ref[:, lanes] = (local_qkv[0, :, lanes] * mixed).astype(BF16)
        cgrad[0, pl.ds(0, TILE), lanes] = ct[:, lanes].astype(F32) * mixed
    own4.wait()
    others(ret_snd.at[1], ret_rcv.at[1], 3).wait_recv()
    for q, lanes in enumerate(strips):
        pgrad = turn_back(ret_rcv.at[1], q)
        cgrad[1, pl.ds(0, TILE), lanes] = pgrad * local_qkv[2, :, lanes]
        cgrad[2, pl.ds(0, TILE), lanes] = pgrad * local_qkv[1, :, lanes]
    edge = cgrad.at[:, pl.ds(0, 8)]
    beyond = cgrad.at[:, pl.ds(TILE, 8)]
    edge_out = remote(edge, beyond, 7, lax.rem(me + count - 1, count))
    edge_in = remote(edge, beyond, 7, me)

    @pl.when(me > 0)
    def _():
        edge_out.start()

    @pl.when(me < count - 1)
    def _():
        edge_in.wait_recv()

    @pl.when(me == count - 1)
    def _():
        cgrad[:, pl.ds(TILE, 8), :] = jnp.zeros((3, 8, cgrad.shape[2]), F32)

    for i in range(3):
        for lanes in strips:
            total = None
            for j in range(reach + 1):
                term = taps[i, pl.ds(j, 1), lanes] * cgrad[i, pl.ds(j, TILE), lanes]
                total = term if total is None else total + term
            sgrad_ref[i, :, lanes] = total.astype(BF16)
    own5.wait()
    others(ret_snd.at[2], ret_rcv.at[2], 4).wait_recv()
    for q, lanes in enumerate(strips):
        fgrad_ref[:, lanes] = turn_back(ret_rcv.at[2], q).astype(BF16)
    own6.wait()
    others(tall, tall, 5).wait_recv()
    by_entry = tall[...].reshape(count, TILE).T
    width = ext.shape[2]
    total = None
    for c in range(CHANS):
        channel = lax.broadcasted_iota(jnp.int32, (count, width), 1)
        owner = lax.broadcasted_iota(jnp.int32, (count, width), 0)
        place = (channel == CHANS * owner + c).astype(F32)
        term = jnp.dot(
            by_entry[c * ENTRIES : (c + 1) * ENTRIES], place,
            precision=lax.Precision.HIGHEST, preferred_element_type=F32,
        )
        total = term if total is None else total + term
    tgrad_ref[...] = total
    others(snd1, rcv1, 0).wait_send()
    others(snd2, rcv2, 1).wait_send()
    for k in range(3):
        others(ret_snd.at[k], ret_rcv.at[k], 2 + k).wait_send()
    others(tall, tall, 5).wait_send()

    @pl.when(me < count - 1)
    def _():
        halo_out.wait_send()

    @pl.when(me > 0)
    def _():
        edge_out.wait_send()


def local(streams, taps, filters, cotangent):
    rows, width = filters.shape
    count = lax.axis_size("ctx")
    assert rows == TILE and width == CHANS * count and count == TILE
    tables = [jnp.asarray(t) for t in make_tables(count, rows)]
    reach = taps.shape[1] - 1
    any_space = pl.BlockSpec(memory_space=pl.ANY)
    vmem = pl.BlockSpec(memory_space=VMEM)
    line = (count, CHANS, TILE)
    scratch = [
        VMEM(streams.shape, BF16), VMEM(filters.shape, BF16), VMEM(cotangent.shape, BF16), VMEM(taps.shape, F32),
        *[VMEM(t.shape, t.dtype) for t in tables],
        VMEM((count, 3, CHANS, TILE), BF16), VMEM((count, 2, CHANS, TILE), BF16),
        VMEM((count, 3, CHANS, TILE), BF16), VMEM((count, 2, CHANS, TILE), BF16),
        VMEM((5, 8 + count * CHANS, TILE), F32),
        VMEM((3, CHANS, reach + 1, count, TILE), F32),
        VMEM((3, CHANS, count, TILE), F32),
        VMEM((3, 2, 2 * count, 2 * TILE), F32),
        VMEM((count * CHANS, TILE), F32),
        VMEM((3,) + line, BF16), VMEM((3,) + line, BF16),
        VMEM((TILE, 8, TILE), F32), VMEM((1, TILE), F32), VMEM((count, 1, TILE), F32),
        VMEM((3, 16, width), BF16),
        VMEM((3, 8 + TILE, width), F32),
        VMEM((3, TILE, width), F32),
        VMEM((3, TILE + 8, width), F32),
        pltpu.SemaphoreType.DMA((9,)), pltpu.SemaphoreType.DMA((6,)),
        pltpu.SemaphoreType.DMA((8,)), pltpu.SemaphoreType.DMA((8,)),
    ]
    gated, sgrad, fgrad, tgrad = pl.pallas_call(
        block_kernel,
        out_shape=[
            jax.ShapeDtypeStruct(cotangent.shape, BF16),
            jax.ShapeDtypeStruct(streams.shape, BF16),
            jax.ShapeDtypeStruct(filters.shape, BF16),
            jax.ShapeDtypeStruct((ENTRIES, width), F32),
        ],
        in_specs=[any_space] * 9 + [pl.BlockSpec(memory_space=pltpu.SMEM)],
        out_specs=[vmem] * 4,
        scratch_shapes=scratch,
        compiler_params=pltpu.CompilerParams(collective_id=0, has_side_effects=True),
    )(streams, filters, cotangent, taps, *tables, taps)
    return gated, sgrad, fgrad, tgrad[: taps.shape[0] * taps.shape[1]].reshape(taps.shape)


def solution(mesh):
    in_specs = (P(None, "ctx", "fft"), P(None, None, "fft"), P("ctx", "fft"), P("ctx", "fft"))
    out_specs = (P("ctx", "fft"), P(None, "ctx", "fft"), P("ctx", "fft"), P(None, None, "fft"))
    return jax.shard_map(local, mesh=mesh, in_specs=in_specs, out_specs=out_specs, check_vma=False)
```

```python
import math

import jax
import jax.numpy as jnp
import numpy as np
from jax import lax
from jax.experimental import pallas as pl
from jax.experimental.pallas import tpu as pltpu
from jax.sharding import PartitionSpec as P

MESH = pl.DeviceIdType.MESH
VMEM = pltpu.VMEM
F32 = jnp.float32
BF16 = jnp.bfloat16
CHANS = 4
TILE = 128
ENTRIES = 24
UNROLL = 7
LATER = (1, 8, 9)


def halves(table):
    high = table.astype(BF16)
    return high, (table - high.astype(np.float64)).astype(BF16)


def make_tables(a_size, b_size):
    k1, a, b, k2 = (np.arange(n, dtype=np.int64) for n in (a_size, a_size, b_size, b_size))
    first = (4 * k1[:, None] + 1) * a[None, :] % (4 * a_size) / (4.0 * a_size)
    twist = (4 * k1[:, None] + 1) * b[None, :] % (4 * a_size * b_size) / (4.0 * a_size * b_size)
    second = b[:, None] * k2[None, :] % b_size / float(b_size)
    first, twist, second = (np.exp(-2j * np.pi * x) for x in (first, twist, second))
    e1 = np.concatenate([first.real, first.imag], 0)
    e2 = np.block([[second.real, second.imag], [-second.imag, second.real]])
    back = np.concatenate([first.real.T, first.imag.T], 1) / (a_size * b_size)
    e1 = np.concatenate(halves(e1), 1)
    e2, e2t, back = (np.stack(halves(x)) for x in (e2, e2.T, back))
    twist = np.stack([np.tile(x, (1, 2)) for x in (twist.real, twist.imag)]).astype(np.float32)
    return e1, e2, e2t, back, twist


def dot(a, b):
    return jnp.dot(a, b, preferred_element_type=F32)


def split(x):
    high = x.astype(BF16)
    return high, (x - high.astype(F32)).astype(BF16)


def turn_back(source, q):
    tile = source[pl.ds(q * TILE // CHANS, TILE // CHANS)].astype(F32).reshape(TILE, TILE)
    return tile.T


def block_kernel(
    streams_hbm, filters_hbm, cot_hbm, taps_hbm, e1_hbm, e2_hbm, e2t_hbm, back_hbm, tw_hbm,
    gated_ref, sgrad_ref, fgrad_raw, tall,
    st, fl, ct, taps, e1, e2, e2t, back, tw,
    snd1, snd2, rcv1, rcv2, own_taps, grid, shifts, qkv, spec, rows, mixed_rows, ret_snd, ret_rcv,
    sums, small, halo, ext, local_qkv, cgrad,
    in_sem, own_sem, send_sem, recv_sem,
):
    count = rcv1.shape[0]
    width = ext.shape[2]
    reach = taps.shape[1] - 1
    scale = 1.0 / math.sqrt(count * TILE)
    me = lax.axis_index("ctx")
    barrier = pltpu.get_barrier_semaphore()

    def remote(source, target, sem, peer):
        return pltpu.make_async_remote_copy(
            source, target, send_sem.at[sem], recv_sem.at[sem], device_id={"ctx": peer}, device_id_type=MESH
        )

    def each_peer(visit):
        def several(block, carry):
            for k in range(UNROLL):
                visit(lax.rem(me + 1 + UNROLL * block + k, count))
            return carry

        blocks = (count - 1) // UNROLL
        lax.fori_loop(0, blocks, several, 0)
        for step in range(1 + UNROLL * blocks, count):
            visit(lax.rem(me + step, count))


    loads = [
        pltpu.make_async_copy(source, target, in_sem.at[i])
        for i, (source, target) in enumerate(
            (
                (streams_hbm, st), (filters_hbm, fl), (cot_hbm, ct), (taps_hbm, taps), (e1_hbm, e1),
                (e2_hbm, e2), (e2t_hbm, e2t), (back_hbm, back), (tw_hbm, tw),
            )
        )
    ]
    for load in loads:
        load.start()

    def greet(peer):
        pl.semaphore_signal(barrier, inc=1, device_id={"ctx": peer}, device_id_type=MESH)

    each_peer(greet)

    def turn_out(source, target):
        for q in range(source.shape[1] // TILE):
            tile = source[:, q * TILE : (q + 1) * TILE].astype(F32).T
            target[pl.ds(q * TILE // CHANS, TILE // CHANS)] = tile.astype(BF16).reshape(-1, CHANS, TILE)

    loads[0].wait()
    turn_out(st.at[1], snd1.at[:, 0])
    turn_out(st.at[2], snd1.at[:, 1])
    loads[1].wait()
    turn_out(fl, snd2.at[0])
    turn_out(st.at[0], snd2.at[1])
    loads[2].wait()
    turn_out(ct, snd2.at[2])
    for load in loads[3:]:
        load.wait()
    for i in range(3):
        for c in range(CHANS):
            chosen = lax.broadcasted_iota(jnp.int32, (reach + 1, width), 1) == CHANS * me + c
            tap = jnp.sum(jnp.where(chosen, taps[i], 0.0), 1, keepdims=True)
            own_taps[c, i, pl.ds(0, reach + 1), :] = jnp.broadcast_to(tap, (reach + 1, TILE))

    def scatter(source, target, sem):
        own = pltpu.make_async_copy(source.at[me], target.at[me], own_sem.at[sem])
        own.start()
        each_peer(lambda peer: remote(source.at[peer], target.at[me], sem, peer).start())
        return own

    def others(source, target, sem):
        return remote(source.at[pl.ds(0, count - 1)], target.at[pl.ds(0, count - 1)], sem, me)

    pl.semaphore_wait(barrier, count - 1)
    halo_out = remote(st.at[:, pl.ds(TILE - 16, 16)], halo, 6, lax.rem(me + 1, count))
    halo_in = remote(st.at[:, pl.ds(TILE - 16, 16)], halo, 6, me)

    @pl.when(me < count - 1)
    def _():
        halo_out.start()

    own1 = scatter(snd1, rcv1, 0)
    own2 = [scatter(snd2.at[k], rcv2.at[k], sem) for k, sem in enumerate(LATER)]

    sums[...] = jnp.zeros_like(sums)
    grid[:, pl.ds(0, 8), :] = jnp.zeros((5, 8, TILE), F32)
    ext[:, pl.ds(8, TILE), :] = st[...].astype(F32)

    @pl.when(me > 0)
    def _():
        halo_in.wait_recv()
        ext[:, pl.ds(0, 8), :] = halo[...].astype(F32)[:, 8:, :]

    @pl.when(me == 0)
    def _():
        ext[:, pl.ds(0, 8), :] = jnp.zeros((3, 8, ext.shape[2]), F32)

    for i in range(3):
        for q in range(ext.shape[2] // TILE):
            lanes = pl.ds(q * TILE, TILE)
            total = None
            for j in range(reach + 1):
                term = taps[i, pl.ds(j, 1), lanes] * ext[i, pl.ds(8 - j, TILE), lanes]
                total = term if total is None else total + term
            local_qkv[i, :, lanes] = total

    lane = lax.broadcasted_iota(jnp.int32, (TILE, TILE), 1)

    def unpack(source, index):
        grid[index, pl.ds(8, count * CHANS), :] = source[...].astype(F32).reshape(count * CHANS, TILE)

    def plane(index, c):
        return grid[index, pl.ds(8 + c, count, stride=CHANS), :]

    def convolve(index, c):
        here = plane(index, c)
        before = grid[index, pl.ds(8 - CHANS + c, count, stride=CHANS), :]
        total = own_taps[c, index, pl.ds(0, 1), :] * here
        for j in range(1, reach + 1):
            moved = pltpu.roll(jnp.where(lane >= TILE - j, before, here), j, 1)
            shifts[index, c, j] = moved
            total = total + own_taps[c, index, pl.ds(j, 1), :] * moved
        qkv[index, c] = total
        return total

    def forward(planes, index, h):
        x = jnp.concatenate(planes, 1)
        y = dot(e1[...], jnp.concatenate([x, x], 0))
        re, im = y[:count], y[count:]
        twr, twi = tw[0], tw[1]
        tre, tim = re * twr - im * twi, re * twi + im * twr
        turned = jnp.concatenate(
            [jnp.concatenate([v[:, n * TILE : (n + 1) * TILE] for v in (tre, tim)], 1) for n in range(2)], 0
        )
        high, low = split(turned)
        spec[index, h] = dot(high, e2[0]) + dot(low, e2[0]) + dot(high, e2[1])

    def spectrum(index, h):
        return spec[index, h, :, pl.ds(0, TILE)], spec[index, h, :, pl.ds(TILE, TILE)]

    def inverse(re, im):
        high, low = split(jnp.concatenate([re, im], 1))
        u = dot(high, e2t[0]) + dot(low, e2t[0]) + dot(high, e2t[1])
        ur = jnp.concatenate([u[:count, :TILE], u[count:, :TILE]], 1)
        ui = jnp.concatenate([u[:count, TILE:], u[count:, TILE:]], 1)
        twr, twi = tw[0], tw[1]
        high, low = split(jnp.concatenate([ur * twr + ui * twi, ui * twr - ur * twi], 0))
        return dot(back[0], high) + dot(back[1], high) + dot(back[0], low)

    def put_rows(h, y):
        for n in range(2):
            rows[pl.ds(2 * h + n, count, stride=CHANS), :] = y[:, n * TILE : (n + 1) * TILE]

    def pack(which):
        ret_snd[which] = rows[...].astype(BF16).reshape(count, CHANS, TILE)

    def tap_sums(index, c, grad):
        for j in range(reach + 1):
            moved = plane(index, c) if j == 0 else shifts[index, c, j]
            part = jnp.sum((grad * moved).reshape(count // 8, 8, TILE), 0)
            sums[c * ENTRIES + index * (reach + 1) + j] = part

    own1.wait()
    others(snd1, rcv1, 0).wait_recv()
    unpack(rcv1.at[:, 0], 1)
    unpack(rcv1.at[:, 1], 2)
    for h in range(2):
        products = [(convolve(1, c) * convolve(2, c)).astype(BF16) for c in (2 * h, 2 * h + 1)]
        forward(products, 0, h)
    own2[0].wait()
    others(snd2.at[0], rcv2.at[0], LATER[0]).wait_recv()
    unpack(rcv2.at[0], 3)
    for h in range(2):
        forward([plane(3, c).astype(BF16) for c in (2 * h, 2 * h + 1)], 1, h)
        pr, pi = spectrum(0, h)
        fr, fi = spectrum(1, h)
        put_rows(h, inverse(pr * fr - pi * fi, pr * fi + pi * fr))
    pack(0)
    own3 = scatter(ret_snd.at[0], ret_rcv.at[0], 2)

    own2[1].wait()
    others(snd2.at[1], rcv2.at[1], LATER[1]).wait_recv()
    unpack(rcv2.at[1], 0)
    for c in range(CHANS):
        convolve(0, c)
        mixed_rows[c] = rows[pl.ds(c, count, stride=CHANS), :].astype(BF16).astype(F32)
    own2[2].wait()
    others(snd2.at[2], rcv2.at[2], LATER[2]).wait_recv()
    unpack(rcv2.at[2], 4)
    for h in range(2):
        forward([(plane(4, c) * qkv[0, c]).astype(BF16) for c in (2 * h, 2 * h + 1)], 2, h)
    for h in range(2):
        fr, fi = spectrum(1, h)
        gr, gi = spectrum(2, h)
        y = inverse(fr * gr + fi * gi, fr * gi - fi * gr)
        put_rows(h, y)
    pack(1)
    own4 = scatter(ret_snd.at[1], ret_rcv.at[1], 3)
    for c in range(CHANS):
        tap_sums(0, c, plane(4, c) * mixed_rows[c])
        pgrad = rows[pl.ds(c, count, stride=CHANS), :].astype(BF16).astype(F32)
        tap_sums(1, c, pgrad * qkv[2, c])
        tap_sums(2, c, pgrad * qkv[1, c])
    entries = jnp.sum(sums[...], 1)
    row = lax.dot_general(
        jnp.ones((8, TILE), F32), entries, (((1,), (1,)), ((), ())),
        precision=lax.Precision.HIGHEST, preferred_element_type=F32,
    )
    small[...] = row[0:1] * scale
    for h in range(2):
        pr, pi = spectrum(0, h)
        gr, gi = spectrum(2, h)
        put_rows(h, inverse(pr * gr + pi * gi, pr * gi - pi * gr) * scale)
    pack(2)
    own5 = pltpu.make_async_copy(ret_snd.at[2].at[me], fgrad_raw.at[me], own_sem.at[4])
    own5.start()
    own6 = pltpu.make_async_copy(small, tall.at[me], own_sem.at[5])
    own6.start()

    def last(peer):
        remote(ret_snd.at[2].at[peer], fgrad_raw.at[me], 4, peer).start()
        remote(small, tall.at[me], 5, peer).start()

    each_peer(last)

    strips = [pl.ds(q * TILE, TILE) for q in range(ext.shape[2] // TILE)]
    own3.wait()
    others(ret_snd.at[0], ret_rcv.at[0], 2).wait_recv()
    for q, lanes in enumerate(strips):
        mixed = turn_back(ret_rcv.at[0], q)
        gated_ref[:, lanes] = (local_qkv[0, :, lanes] * mixed).astype(BF16)
        cgrad[0, pl.ds(0, TILE), lanes] = ct[:, lanes].astype(F32) * mixed
    own4.wait()
    others(ret_snd.at[1], ret_rcv.at[1], 3).wait_recv()
    for q, lanes in enumerate(strips):
        pgrad = turn_back(ret_rcv.at[1], q)
        cgrad[1, pl.ds(0, TILE), lanes] = pgrad * local_qkv[2, :, lanes]
        cgrad[2, pl.ds(0, TILE), lanes] = pgrad * local_qkv[1, :, lanes]
    edge = cgrad.at[:, pl.ds(0, 8)]
    beyond = cgrad.at[:, pl.ds(TILE, 8)]
    edge_out = remote(edge, beyond, 7, lax.rem(me + count - 1, count))
    edge_in = remote(edge, beyond, 7, me)

    @pl.when(me > 0)
    def _():
        edge_out.start()

    def correlate(first, number):
        for i in range(3):
            for lanes in strips:
                total = None
                for j in range(reach + 1):
                    term = taps[i, pl.ds(j, 1), lanes] * cgrad[i, pl.ds(first + j, number), lanes]
                    total = term if total is None else total + term
                sgrad_ref[i, pl.ds(first, number), lanes] = total.astype(BF16)

    correlate(0, TILE - 16)

    @pl.when(me < count - 1)
    def _():
        edge_in.wait_recv()

    @pl.when(me == count - 1)
    def _():
        cgrad[:, pl.ds(TILE, 8), :] = jnp.zeros((3, 8, width), F32)

    correlate(TILE - 16, 16)
    own5.wait()
    others(ret_snd.at[2], fgrad_raw, 4).wait_recv()
    own6.wait()
    others(tall, tall, 5).wait_recv()
    others(snd1, rcv1, 0).wait_send()
    for k, sem in enumerate(LATER):
        others(snd2.at[k], rcv2.at[k], sem).wait_send()
    for k in range(2):
        others(ret_snd.at[k], ret_rcv.at[k], 2 + k).wait_send()
    others(ret_snd.at[2], fgrad_raw, 4).wait_send()
    others(tall, tall, 5).wait_send()

    @pl.when(me < count - 1)
    def _():
        halo_out.wait_send()

    @pl.when(me > 0)
    def _():
        edge_out.wait_send()


def result_kernel(
    gated, sgrad, fgrad_raw, tall, gated_hbm, sgrad_hbm, fgrad_hbm, tgrad_hbm, fgrad, tgrad, spread, sem
):
    count = tall.shape[0]
    terms = tgrad.shape[1]
    stores = [
        pltpu.make_async_copy(source, target, sem.at[i])
        for i, (source, target) in enumerate(
            ((gated, gated_hbm), (sgrad, sgrad_hbm), (fgrad, fgrad_hbm), (tgrad, tgrad_hbm))
        )
    ]
    stores[0].start()
    stores[1].start()
    for q in range(fgrad.shape[1] // TILE):
        fgrad[:, q * TILE : (q + 1) * TILE] = turn_back(fgrad_raw, q).astype(BF16)
    stores[2].start()
    entries = tall[...].reshape(count, TILE)
    for c in range(CHANS):
        moved = pltpu.roll(entries, TILE - c * ENTRIES, 1) if c else entries
        spread[pl.ds(c, count, stride=CHANS), :] = moved
    for q in range(fgrad.shape[1] // TILE):
        by_entry = spread[q * TILE : (q + 1) * TILE, :].T
        for i in range(tgrad.shape[0]):
            tgrad[i, :, q * TILE : (q + 1) * TILE] = by_entry[i * terms : (i + 1) * terms]
    stores[3].start()
    for store in stores:
        store.wait()


def local(streams, taps, filters, cotangent):
    rows, width = filters.shape
    count = lax.axis_size("ctx")
    assert rows == TILE and width == CHANS * count and count == TILE
    tables = [jnp.asarray(t) for t in make_tables(count, rows)]
    reach = taps.shape[1] - 1
    hbm = pl.BlockSpec(memory_space=pltpu.HBM)
    vmem = pl.BlockSpec(memory_space=VMEM)
    line = (count, CHANS, TILE)
    pair = (count, 2, CHANS, TILE)
    scratch = [
        VMEM(streams.shape, BF16), VMEM(filters.shape, BF16), VMEM(cotangent.shape, BF16), VMEM(taps.shape, F32),
        *[VMEM(t.shape, t.dtype) for t in tables],
        VMEM(pair, BF16), VMEM((3,) + line, BF16), VMEM(pair, BF16), VMEM((3,) + line, BF16),
        VMEM((CHANS, 3, 8, TILE), F32),
        VMEM((5, 8 + count * CHANS, TILE), F32),
        VMEM((3, CHANS, reach + 1, count, TILE), F32),
        VMEM((3, CHANS, count, TILE), F32),
        VMEM((3, 2, 2 * count, 2 * TILE), F32),
        VMEM((count * CHANS, TILE), F32), VMEM((CHANS, count, TILE), F32),
        VMEM((3,) + line, BF16), VMEM((2,) + line, BF16),
        VMEM((TILE, 8, TILE), F32), VMEM((1, TILE), F32),
        VMEM((3, 16, width), BF16),
        VMEM((3, 8 + TILE, width), F32),
        VMEM((3, TILE, width), F32),
        VMEM((3, TILE + 8, width), F32),
        pltpu.SemaphoreType.DMA((9,)), pltpu.SemaphoreType.DMA((10,)),
        pltpu.SemaphoreType.DMA((10,)), pltpu.SemaphoreType.DMA((10,)),
    ]
    parts = pl.pallas_call(
        block_kernel,
        out_shape=[
            jax.ShapeDtypeStruct(cotangent.shape, BF16),
            jax.ShapeDtypeStruct(streams.shape, BF16),
            jax.ShapeDtypeStruct(line, BF16),
            jax.ShapeDtypeStruct((count, 1, TILE), F32),
        ],
        in_specs=[hbm] * 9,
        out_specs=[vmem] * 4,
        scratch_shapes=scratch,
        compiler_params=pltpu.CompilerParams(
            collective_id=0, has_side_effects=True, vmem_limit_bytes=40 << 20
        ),
    )(*[pltpu.with_memory_space_constraint(x, pltpu.HBM) for x in (streams, filters, cotangent, taps, *tables)])
    return pl.pallas_call(
        result_kernel,
        out_shape=[
            jax.ShapeDtypeStruct(cotangent.shape, BF16),
            jax.ShapeDtypeStruct(streams.shape, BF16),
            jax.ShapeDtypeStruct(filters.shape, BF16),
            jax.ShapeDtypeStruct(taps.shape, F32),
        ],
        in_specs=[vmem] * 4,
        out_specs=[hbm] * 4,
        scratch_shapes=[
            VMEM(filters.shape, BF16), VMEM(taps.shape, F32), VMEM((count * CHANS, TILE), F32),
            pltpu.SemaphoreType.DMA((4,)),
        ],
        compiler_params=pltpu.CompilerParams(vmem_limit_bytes=8 << 20),
    )(*parts)


def solution(mesh):
    in_specs = (P(None, "ctx", "fft"), P(None, None, "fft"), P("ctx", "fft"), P("ctx", "fft"))
    out_specs = (P("ctx", "fft"), P(None, "ctx", "fft"), P("ctx", "fft"), P(None, None, "fft"))
    return jax.shard_map(local, mesh=mesh, in_specs=in_specs, out_specs=out_specs, check_vma=False)
```

```python
import math

import jax
import jax.numpy as jnp
import numpy as np
from jax import lax
from jax.experimental import pallas as pl
from jax.experimental.pallas import tpu as pltpu
from jax.sharding import PartitionSpec as P

MESH = pl.DeviceIdType.MESH
VMEM = pltpu.VMEM
F32 = jnp.float32
BF16 = jnp.bfloat16
CHANS = 4
TILE = 128
ENTRIES = 24
Y_SIZE, Z_SIZE, X_SIZE = 8, 8, 2
LATER = (1, 8, 9)


def halves(table):
    high = table.astype(BF16)
    return high, (table - high.astype(np.float64)).astype(BF16)


def make_tables(a_size, b_size):
    k1, a, b, k2 = (np.arange(n, dtype=np.int64) for n in (a_size, a_size, b_size, b_size))
    first = (4 * k1[:, None] + 1) * a[None, :] % (4 * a_size) / (4.0 * a_size)
    twist = (4 * k1[:, None] + 1) * b[None, :] % (4 * a_size * b_size) / (4.0 * a_size * b_size)
    second = b[:, None] * k2[None, :] % b_size / float(b_size)
    first, twist, second = (np.exp(-2j * np.pi * x) for x in (first, twist, second))
    e1 = np.concatenate([first.real, first.imag], 0)
    e2 = np.block([[second.real, second.imag], [-second.imag, second.real]])
    back = np.concatenate([first.real.T, first.imag.T], 1) / (a_size * b_size)
    e1 = np.concatenate(halves(e1), 1)
    e2, e2t, back = (np.stack(halves(x)) for x in (e2, e2.T, back))
    twist = np.stack([np.tile(x, (1, 2)) for x in (twist.real, twist.imag)]).astype(np.float32)
    return e1, e2, e2t, back, twist


def dot(a, b):
    return jnp.dot(a, b, preferred_element_type=F32)


def split(x):
    high = x.astype(BF16)
    return high, (x - high.astype(F32)).astype(BF16)


def turn_back(source, q):
    tile = source[pl.ds(q * TILE // CHANS, TILE // CHANS)].astype(F32).reshape(TILE, TILE)
    return tile.T


def block_kernel(
    streams_hbm, filters_hbm, cot_hbm, taps_hbm, e1_hbm, e2_hbm, e2t_hbm, back_hbm, tw_hbm,
    gated_ref, sgrad_ref, fgrad_ref, tall,
    st, fl, ct, taps, e1, e2, e2t, back, tw,
    snd1, snd2, rcv1, rcv2, own_taps, grid, shifts, qkv, spec, rows, mixed_rows, ret_snd, ret_rcv,
    sums, small, halo, ext, local_qkv, cgrad,
    in_sem, own_sem, send_sem, recv_sem,
):
    count = rcv1.shape[0]
    width = ext.shape[2]
    reach = taps.shape[1] - 1
    scale = 1.0 / math.sqrt(count * TILE)
    me = lax.axis_index("ctx")
    barrier = pltpu.get_barrier_semaphore()

    def remote(source, target, sem, peer):
        return pltpu.make_async_remote_copy(
            source, target, send_sem.at[sem], recv_sem.at[sem], device_id={"ctx": peer}, device_id_type=MESH
        )

    zx_count = Z_SIZE * X_SIZE
    y, zx = me // zx_count, lax.rem(me, zx_count)
    z, x = zx // X_SIZE, lax.rem(zx, X_SIZE)
    planes = [
        lax.rem(z + dz, Z_SIZE) * X_SIZE + lax.rem(x + dx, X_SIZE)
        for dz in (4, 3, 5, 2, 6, 1, 7, 0)
        for dx in (1, 0)
    ]

    def each_peer(visit):
        def row(step, carry):
            half = (step + 1) // 2
            dy = 4 + half - 2 * half * lax.rem(step, 2)
            base = lax.rem(y + dy, Y_SIZE) * zx_count
            for plane_at in planes:
                visit(base + plane_at)
            return carry

        lax.fori_loop(0, Y_SIZE - 1, row, 0)
        for plane_at in planes[:-1]:
            visit(y * zx_count + plane_at)

    loads = [
        pltpu.make_async_copy(source, target, in_sem.at[i])
        for i, (source, target) in enumerate(
            (
                (streams_hbm, st), (filters_hbm, fl), (cot_hbm, ct), (taps_hbm, taps), (e1_hbm, e1),
                (e2_hbm, e2), (e2t_hbm, e2t), (back_hbm, back), (tw_hbm, tw),
            )
        )
    ]
    for load in loads:
        load.start()

    def greet(peer):
        pl.semaphore_signal(barrier, inc=1, device_id={"ctx": peer}, device_id_type=MESH)

    each_peer(greet)

    def turn_out(source, target):
        for q in range(source.shape[1] // TILE):
            tile = source[:, q * TILE : (q + 1) * TILE].astype(F32).T
            target[pl.ds(q * TILE // CHANS, TILE // CHANS)] = tile.astype(BF16).reshape(-1, CHANS, TILE)

    loads[0].wait()
    turn_out(st.at[1], snd1.at[:, 0])
    turn_out(st.at[2], snd1.at[:, 1])
    loads[1].wait()
    turn_out(fl, snd2.at[0])
    loads[2].wait()
    lane = lax.broadcasted_iota(jnp.int32, (TILE, TILE), 1)
    low = lax.rem(lane, CHANS) < 2
    for q in range(width // TILE):
        lanes = pl.ds(q * TILE, TILE)
        place = pl.ds(q * TILE // CHANS, TILE // CHANS)
        first, second = st[0, :, lanes].astype(F32), ct[:, lanes].astype(F32)
        tiles = (
            jnp.where(low, first, pltpu.roll(second, 2, 1)),
            jnp.where(low, pltpu.roll(first, TILE - 2, 1), second),
        )
        for h, tile in enumerate(tiles):
            snd2.at[1 + h][place] = tile.T.astype(BF16).reshape(-1, CHANS, TILE)
    for load in loads[3:]:
        load.wait()
    for i in range(3):
        for c in range(CHANS):
            chosen = lax.broadcasted_iota(jnp.int32, (reach + 1, width), 1) == CHANS * me + c
            tap = jnp.sum(jnp.where(chosen, taps[i], 0.0), 1, keepdims=True)
            own_taps[c, i, pl.ds(0, reach + 1), :] = jnp.broadcast_to(tap, (reach + 1, TILE))

    def scatter(source, target, sem):
        own = pltpu.make_async_copy(source.at[me], target.at[me], own_sem.at[sem])
        own.start()
        each_peer(lambda peer: remote(source.at[peer], target.at[me], sem, peer).start())
        return own

    def others(source, target, sem):
        return remote(source.at[pl.ds(0, count - 1)], target.at[pl.ds(0, count - 1)], sem, me)

    pl.semaphore_wait(barrier, count - 1)
    halo_out = remote(st.at[:, pl.ds(TILE - 16, 16)], halo, 6, lax.rem(me + 1, count))
    halo_in = remote(st.at[:, pl.ds(TILE - 16, 16)], halo, 6, me)

    @pl.when(me < count - 1)
    def _():
        halo_out.start()

    own1 = scatter(snd1, rcv1, 0)
    own2 = [scatter(snd2.at[k], rcv2.at[k], sem) for k, sem in enumerate(LATER)]

    sums[...] = jnp.zeros_like(sums)
    grid[:, pl.ds(0, 8), :] = jnp.zeros((5, 8, TILE), F32)
    ext[:, pl.ds(8, TILE), :] = st[...].astype(F32)

    @pl.when(me > 0)
    def _():
        halo_in.wait_recv()
        ext[:, pl.ds(0, 8), :] = halo[...].astype(F32)[:, 8:, :]

    @pl.when(me == 0)
    def _():
        ext[:, pl.ds(0, 8), :] = jnp.zeros((3, 8, ext.shape[2]), F32)

    for i in range(3):
        for q in range(ext.shape[2] // TILE):
            lanes = pl.ds(q * TILE, TILE)
            total = None
            for j in range(reach + 1):
                term = taps[i, pl.ds(j, 1), lanes] * ext[i, pl.ds(8 - j, TILE), lanes]
                total = term if total is None else total + term
            local_qkv[i, :, lanes] = total

    def slot(index, c):
        if index in (1, 2, 3):
            return index, c
        return (0, 4)[c // 2], c % 2 + (2 if index == 4 else 0)

    def unpack(source, index):
        grid[index, pl.ds(8, count * CHANS), :] = source[...].astype(F32).reshape(count * CHANS, TILE)

    def plane(index, c):
        block, line = slot(index, c)
        return grid[block, pl.ds(8 + line, count, stride=CHANS), :]

    def convolve(index, c):
        here = plane(index, c)
        block, line = slot(index, c)
        before = grid[block, pl.ds(8 - CHANS + line, count, stride=CHANS), :]
        total = own_taps[c, index, pl.ds(0, 1), :] * here
        for j in range(1, reach + 1):
            moved = pltpu.roll(jnp.where(lane >= TILE - j, before, here), j, 1)
            shifts[index, c, j] = moved
            total = total + own_taps[c, index, pl.ds(j, 1), :] * moved
        qkv[index, c] = total
        return total

    def forward(planes, index, h):
        x = jnp.concatenate(planes, 1)
        y = dot(e1[...], jnp.concatenate([x, x], 0))
        re, im = y[:count], y[count:]
        twr, twi = tw[0], tw[1]
        tre, tim = re * twr - im * twi, re * twi + im * twr
        turned = jnp.concatenate(
            [jnp.concatenate([v[:, n * TILE : (n + 1) * TILE] for v in (tre, tim)], 1) for n in range(2)], 0
        )
        high, low = split(turned)
        spec[index, h] = dot(high, e2[0]) + dot(low, e2[0]) + dot(high, e2[1])

    def spectrum(index, h):
        return spec[index, h, :, pl.ds(0, TILE)], spec[index, h, :, pl.ds(TILE, TILE)]

    def inverse(re, im):
        high, low = split(jnp.concatenate([re, im], 1))
        u = dot(high, e2t[0]) + dot(low, e2t[0]) + dot(high, e2t[1])
        ur = jnp.concatenate([u[:count, :TILE], u[count:, :TILE]], 1)
        ui = jnp.concatenate([u[:count, TILE:], u[count:, TILE:]], 1)
        twr, twi = tw[0], tw[1]
        high, low = split(jnp.concatenate([ur * twr + ui * twi, ui * twr - ur * twi], 0))
        return dot(back[0], high) + dot(back[1], high) + dot(back[0], low)

    def put_rows(h, values):
        for n in range(2):
            rows[pl.ds(2 * h + n, count, stride=CHANS), :] = values[:, n * TILE : (n + 1) * TILE]

    def pack(which):
        ret_snd[which] = rows[...].astype(BF16).reshape(count, CHANS, TILE)

    def tap_sums(index, c, grad):
        for j in range(reach + 1):
            moved = plane(index, c) if j == 0 else shifts[index, c, j]
            part = jnp.sum((grad * moved).reshape(count // 8, 8, TILE), 0)
            sums[c * ENTRIES + index * (reach + 1) + j] = part

    own1.wait()
    others(snd1, rcv1, 0).wait_recv()
    unpack(rcv1.at[:, 0], 1)
    unpack(rcv1.at[:, 1], 2)
    for h in range(2):
        products = [(convolve(1, c) * convolve(2, c)).astype(BF16) for c in (2 * h, 2 * h + 1)]
        forward(products, 0, h)
    own2[0].wait()
    others(snd2.at[0], rcv2.at[0], LATER[0]).wait_recv()
    unpack(rcv2.at[0], 3)
    for h in range(2):
        forward([plane(3, c).astype(BF16) for c in (2 * h, 2 * h + 1)], 1, h)
        pr, pi = spectrum(0, h)
        fr, fi = spectrum(1, h)
        put_rows(h, inverse(pr * fr - pi * fi, pr * fi + pi * fr))
    pack(0)
    own3 = scatter(ret_snd.at[0], ret_rcv.at[0], 2)

    for c in range(CHANS):
        mixed_rows[c] = rows[pl.ds(c, count, stride=CHANS), :].astype(BF16).astype(F32)
    own4 = []
    for h in range(2):
        pair = (2 * h, 2 * h + 1)
        own2[1 + h].wait()
        others(snd2.at[1 + h], rcv2.at[1 + h], LATER[1 + h]).wait_recv()
        unpack(rcv2.at[1 + h], (0, 4)[h])
        forward([(plane(4, c) * convolve(0, c)).astype(BF16) for c in pair], 2, h)
        pr, pi = spectrum(0, h)
        fr, fi = spectrum(1, h)
        gr, gi = spectrum(2, h)
        put_rows(0, inverse(fr * gr + fi * gi, fr * gi - fi * gr))
        put_rows(1, inverse(pr * gr + pi * gi, pr * gi - pi * gr) * scale)
        pack(1 + h)
        own4.append(scatter(ret_snd.at[1 + h], ret_rcv.at[1 + h], 3 + h))
        for n, c in enumerate(pair):
            tap_sums(0, c, plane(4, c) * mixed_rows[c])
            pgrad = rows[pl.ds(n, count, stride=CHANS), :].astype(BF16).astype(F32)
            tap_sums(1, c, pgrad * qkv[2, c])
            tap_sums(2, c, pgrad * qkv[1, c])
    entries = jnp.sum(sums[...], 1)
    row = lax.dot_general(
        jnp.ones((8, TILE), F32), entries, (((1,), (1,)), ((), ())),
        precision=lax.Precision.HIGHEST, preferred_element_type=F32,
    )
    small[...] = row[0:1] * scale
    own6 = pltpu.make_async_copy(small, tall.at[me], own_sem.at[5])
    own6.start()
    each_peer(lambda peer: remote(small, tall.at[me], 5, peer).start())

    strips = [pl.ds(q * TILE, TILE) for q in range(width // TILE)]

    def edges(part, sem):
        inner, beyond = cgrad.at[part, pl.ds(0, 8)], cgrad.at[part, pl.ds(TILE, 8)]
        return remote(inner, beyond, sem, lax.rem(me + count - 1, count)), remote(inner, beyond, sem, me)

    def send_edges(edge_out):
        @pl.when(me > 0)
        def _():
            edge_out.start()

    def get_edges(edge_in):
        @pl.when(me < count - 1)
        def _():
            edge_in.wait_recv()

    def correlate(streams, first, number):
        for i in streams:
            for lanes in strips:
                total = None
                for j in range(reach + 1):
                    term = taps[i, pl.ds(j, 1), lanes] * cgrad[i, pl.ds(first + j, number), lanes]
                    total = term if total is None else total + term
                sgrad_ref[i, pl.ds(first, number), lanes] = total.astype(BF16)

    @pl.when(me == count - 1)
    def _():
        cgrad[:, pl.ds(TILE, 8), :] = jnp.zeros((3, 8, width), F32)

    edge_out0, edge_in0 = edges(pl.ds(0, 1), 7)
    edge_out1, edge_in1 = edges(pl.ds(1, 2), 2 + 8)
    own3.wait()
    others(ret_snd.at[0], ret_rcv.at[0], 2).wait_recv()
    for q, lanes in enumerate(strips):
        mixed = turn_back(ret_rcv.at[0], q)
        gated_ref[:, lanes] = (local_qkv[0, :, lanes] * mixed).astype(BF16)
        cgrad[0, pl.ds(0, TILE), lanes] = ct[:, lanes].astype(F32) * mixed
    send_edges(edge_out0)
    correlate((0,), 0, TILE - 16)
    for h in range(2):
        own4[h].wait()
        others(ret_snd.at[1 + h], ret_rcv.at[1 + h], 3 + h).wait_recv()
    for q, lanes in enumerate(strips):
        pgrad = jnp.where(low, turn_back(ret_rcv.at[1], q), pltpu.roll(turn_back(ret_rcv.at[2], q), 2, 1))
        cgrad[1, pl.ds(0, TILE), lanes] = pgrad * local_qkv[2, :, lanes]
        cgrad[2, pl.ds(0, TILE), lanes] = pgrad * local_qkv[1, :, lanes]
    send_edges(edge_out1)
    for q, lanes in enumerate(strips):
        fgrad = jnp.where(low, pltpu.roll(turn_back(ret_rcv.at[1], q), TILE - 2, 1), turn_back(ret_rcv.at[2], q))
        fgrad_ref[:, lanes] = fgrad.astype(BF16)
    correlate((1, 2), 0, TILE - 16)
    get_edges(edge_in0)
    correlate((0,), TILE - 16, 16)
    get_edges(edge_in1)
    correlate((1, 2), TILE - 16, 16)
    own6.wait()
    others(tall, tall, 5).wait_recv()
    others(snd1, rcv1, 0).wait_send()
    for k, sem in enumerate(LATER):
        others(snd2.at[k], rcv2.at[k], sem).wait_send()
    for k in range(3):
        others(ret_snd.at[k], ret_rcv.at[k], 2 + k).wait_send()
    others(tall, tall, 5).wait_send()

    @pl.when(me < count - 1)
    def _():
        halo_out.wait_send()

    @pl.when(me > 0)
    def _():
        edge_out0.wait_send()
        edge_out1.wait_send()


def result_kernel(
    gated, sgrad, fgrad, tall, gated_hbm, sgrad_hbm, fgrad_hbm, tgrad_hbm, tgrad, spread, sem
):
    count = tall.shape[0]
    terms = tgrad.shape[1]
    stores = [
        pltpu.make_async_copy(source, target, sem.at[i])
        for i, (source, target) in enumerate(
            ((gated, gated_hbm), (sgrad, sgrad_hbm), (fgrad, fgrad_hbm), (tgrad, tgrad_hbm))
        )
    ]
    for store in stores[:3]:
        store.start()
    entries = tall[...].reshape(count, TILE)
    for c in range(CHANS):
        moved = pltpu.roll(entries, TILE - c * ENTRIES, 1) if c else entries
        spread[pl.ds(c, count, stride=CHANS), :] = moved
    for q in range(fgrad.shape[1] // TILE):
        by_entry = spread[q * TILE : (q + 1) * TILE, :].T
        for i in range(tgrad.shape[0]):
            tgrad[i, :, q * TILE : (q + 1) * TILE] = by_entry[i * terms : (i + 1) * terms]
    stores[3].start()
    for store in stores:
        store.wait()


def local(streams, taps, filters, cotangent):
    rows, width = filters.shape
    count = lax.axis_size("ctx")
    assert rows == TILE and width == CHANS * count and count == TILE == Y_SIZE * Z_SIZE * X_SIZE
    tables = [jnp.asarray(t) for t in make_tables(count, rows)]
    reach = taps.shape[1] - 1
    hbm = pl.BlockSpec(memory_space=pltpu.HBM)
    vmem = pl.BlockSpec(memory_space=VMEM)
    line = (count, CHANS, TILE)
    pair = (count, 2, CHANS, TILE)
    scratch = [
        VMEM(streams.shape, BF16), VMEM(filters.shape, BF16), VMEM(cotangent.shape, BF16), VMEM(taps.shape, F32),
        *[VMEM(t.shape, t.dtype) for t in tables],
        VMEM(pair, BF16), VMEM((3,) + line, BF16), VMEM(pair, BF16), VMEM((3,) + line, BF16),
        VMEM((CHANS, 3, 8, TILE), F32),
        VMEM((5, 8 + count * CHANS, TILE), F32),
        VMEM((3, CHANS, reach + 1, count, TILE), F32),
        VMEM((3, CHANS, count, TILE), F32),
        VMEM((3, 2, 2 * count, 2 * TILE), F32),
        VMEM((count * CHANS, TILE), F32), VMEM((CHANS, count, TILE), F32),
        VMEM((3,) + line, BF16), VMEM((3,) + line, BF16),
        VMEM((TILE, 8, TILE), F32), VMEM((1, TILE), F32),
        VMEM((3, 16, width), BF16),
        VMEM((3, 8 + TILE, width), F32),
        VMEM((3, TILE, width), F32),
        VMEM((3, TILE + 8, width), F32),
        pltpu.SemaphoreType.DMA((9,)), pltpu.SemaphoreType.DMA((10,)),
        pltpu.SemaphoreType.DMA((11,)), pltpu.SemaphoreType.DMA((11,)),
    ]
    parts = pl.pallas_call(
        block_kernel,
        out_shape=[
            jax.ShapeDtypeStruct(cotangent.shape, BF16),
            jax.ShapeDtypeStruct(streams.shape, BF16),
            jax.ShapeDtypeStruct(filters.shape, BF16),
            jax.ShapeDtypeStruct((count, 1, TILE), F32),
        ],
        in_specs=[hbm] * 9,
        out_specs=[vmem] * 4,
        scratch_shapes=scratch,
        compiler_params=pltpu.CompilerParams(
            collective_id=0, has_side_effects=True, vmem_limit_bytes=40 << 20
        ),
    )(*[pltpu.with_memory_space_constraint(x, pltpu.HBM) for x in (streams, filters, cotangent, taps, *tables)])
    return pl.pallas_call(
        result_kernel,
        out_shape=[
            jax.ShapeDtypeStruct(cotangent.shape, BF16),
            jax.ShapeDtypeStruct(streams.shape, BF16),
            jax.ShapeDtypeStruct(filters.shape, BF16),
            jax.ShapeDtypeStruct(taps.shape, F32),
        ],
        in_specs=[vmem] * 4,
        out_specs=[hbm] * 4,
        scratch_shapes=[
            VMEM(taps.shape, F32), VMEM((count * CHANS, TILE), F32),
            pltpu.SemaphoreType.DMA((4,)),
        ],
        compiler_params=pltpu.CompilerParams(vmem_limit_bytes=8 << 20),
    )(*parts)


def solution(mesh):
    in_specs = (P(None, "ctx", "fft"), P(None, None, "fft"), P("ctx", "fft"), P("ctx", "fft"))
    out_specs = (P("ctx", "fft"), P(None, "ctx", "fft"), P("ctx", "fft"), P(None, None, "fft"))
    return jax.shard_map(local, mesh=mesh, in_specs=in_specs, out_specs=out_specs, check_vma=False)
```

```python
import math

import jax
import jax.numpy as jnp
import numpy as np
from jax import lax
from jax.experimental import pallas as pl
from jax.experimental.pallas import tpu as pltpu
from jax.sharding import PartitionSpec as P

MESH = pl.DeviceIdType.MESH
VMEM = pltpu.VMEM
F32 = jnp.float32
BF16 = jnp.bfloat16
CHANS = 4
TILE = 128
ENTRIES = 32
AHEAD = 24
Y_SIZE, Z_SIZE, X_SIZE = 8, 8, 2
LATER = (1, 8, 10)


def halves(table):
    high = table.astype(BF16)
    return high, (table - high.astype(np.float64)).astype(BF16)


def make_tables(a_size, b_size):
    k1, a, b, k2 = (np.arange(n, dtype=np.int64) for n in (a_size, a_size, b_size, b_size))
    first = (4 * k1[:, None] + 1) * a[None, :] % (4 * a_size) / (4.0 * a_size)
    twist = (4 * k1[:, None] + 1) * b[None, :] % (4 * a_size * b_size) / (4.0 * a_size * b_size)
    second = b[:, None] * k2[None, :] % b_size / float(b_size)
    first, twist, second = (np.exp(-2j * np.pi * x) for x in (first, twist, second))
    e1 = np.concatenate([first.real, first.imag], 0)
    e2 = np.block([[second.real, second.imag], [-second.imag, second.real]])
    back = np.concatenate([first.real.T, first.imag.T], 1) / (a_size * b_size)
    e1 = np.concatenate(halves(e1), 1)
    e2, e2t, back = (np.stack(halves(x)) for x in (e2, e2.T, back))
    twist = np.stack([np.tile(x, (1, 2)) for x in (twist.real, twist.imag)]).astype(np.float32)
    return e1, e2, e2t, back, twist


def dot(a, b):
    return jnp.dot(a, b, preferred_element_type=F32)


def split(x):
    high = x.astype(BF16)
    return high, (x - high.astype(F32)).astype(BF16)


def turn_back(source, q):
    tile = source[pl.ds(q * TILE // CHANS, TILE // CHANS)].astype(F32).reshape(TILE, TILE)
    return tile.T


def block_kernel(
    streams_hbm, filters_hbm, cot_hbm, taps_hbm, e1_hbm, e2_hbm, e2t_hbm, back_hbm, tw_hbm,
    gated_ref, sgrad_ref, fgrad_ref, tgrad_ref,
    st, fl, ct, taps, e1, e2, e2t, back, tw,
    snd1, snd2, rcv1, rcv2, own_taps, grid, shifts, qkv, spec, rows, mixed_rows, pgrad_rows, ret_snd, ret_rcv,
    sums, small, tall, spread, halo, halo_next, ext, local_qkv, cgrad,
    in_sem, own_sem, send_sem, recv_sem,
):
    count = rcv1.shape[0]
    width = ext.shape[2]
    reach = taps.shape[1] - 1
    scale = 1.0 / math.sqrt(count * TILE)
    me = lax.axis_index("ctx")
    barrier = pltpu.get_barrier_semaphore()

    def remote(source, target, sem, peer):
        return pltpu.make_async_remote_copy(
            source, target, send_sem.at[sem], recv_sem.at[sem], device_id={"ctx": peer}, device_id_type=MESH
        )

    zx_count = Z_SIZE * X_SIZE
    y, zx = me // zx_count, lax.rem(me, zx_count)
    z, x = zx // X_SIZE, lax.rem(zx, X_SIZE)
    planes = [
        lax.rem(z + dz, Z_SIZE) * X_SIZE + lax.rem(x + dx, X_SIZE)
        for dz in (4, 3, 5, 2, 6, 1, 7, 0)
        for dx in (1, 0)
    ]

    def each_peer(visit):
        def row(step, carry):
            half = (step + 1) // 2
            dy = 4 + half - 2 * half * lax.rem(step, 2)
            base = lax.rem(y + dy, Y_SIZE) * zx_count
            for plane_at in planes:
                visit(base + plane_at)
            return carry

        lax.fori_loop(0, Y_SIZE - 1, row, 0)
        for plane_at in planes[:-1]:
            visit(y * zx_count + plane_at)

    loads = [
        pltpu.make_async_copy(source, target, in_sem.at[i])
        for i, (source, target) in enumerate(
            (
                (streams_hbm, st), (filters_hbm, fl), (cot_hbm, ct), (taps_hbm, taps), (e1_hbm, e1),
                (e2_hbm, e2), (e2t_hbm, e2t), (back_hbm, back), (tw_hbm, tw),
            )
        )
    ]
    for load in loads:
        load.start()

    def greet(peer):
        pl.semaphore_signal(barrier, inc=1, device_id={"ctx": peer}, device_id_type=MESH)

    each_peer(greet)

    def turn_out(source, target):
        for q in range(source.shape[1] // TILE):
            tile = source[:, q * TILE : (q + 1) * TILE].astype(F32).T
            target[pl.ds(q * TILE // CHANS, TILE // CHANS)] = tile.astype(BF16).reshape(-1, CHANS, TILE)

    loads[0].wait()
    turn_out(st.at[1], snd1.at[:, 0])
    turn_out(st.at[2], snd1.at[:, 1])
    loads[1].wait()
    turn_out(fl, snd2.at[0])
    loads[2].wait()
    lane = lax.broadcasted_iota(jnp.int32, (TILE, TILE), 1)
    low = lax.rem(lane, CHANS) < 2
    for q in range(width // TILE):
        lanes = pl.ds(q * TILE, TILE)
        place = pl.ds(q * TILE // CHANS, TILE // CHANS)
        first, second = st[0, :, lanes].astype(F32), ct[:, lanes].astype(F32)
        tiles = (
            jnp.where(low, first, pltpu.roll(second, 2, 1)),
            jnp.where(low, pltpu.roll(first, TILE - 2, 1), second),
        )
        for h, tile in enumerate(tiles):
            snd2.at[1 + h][place] = tile.T.astype(BF16).reshape(-1, CHANS, TILE)
    for load in loads[3:]:
        load.wait()
    for i in range(3):
        for c in range(CHANS):
            chosen = lax.broadcasted_iota(jnp.int32, (reach + 1, width), 1) == CHANS * me + c
            tap = jnp.sum(jnp.where(chosen, taps[i], 0.0), 1, keepdims=True)
            own_taps[c, i, pl.ds(0, reach + 1), :] = jnp.broadcast_to(tap, (reach + 1, TILE))

    def scatter(source, target, sem):
        own = pltpu.make_async_copy(source.at[me], target.at[me], own_sem.at[sem])
        own.start()
        each_peer(lambda peer: remote(source.at[peer], target.at[me], sem, peer).start())
        return own

    def others(source, target, sem):
        return remote(source.at[pl.ds(0, count - 1)], target.at[pl.ds(0, count - 1)], sem, me)

    pl.semaphore_wait(barrier, count - 1)
    halo_out = remote(st.at[:, pl.ds(TILE - 16, 16)], halo, 6, lax.rem(me + 1, count))
    halo_in = remote(st.at[:, pl.ds(TILE - 16, 16)], halo, 6, me)

    next_out = remote(st.at[pl.ds(1, 2), pl.ds(0, 16)], halo_next, 4 + 5, lax.rem(me + count - 1, count))
    next_in = remote(st.at[pl.ds(1, 2), pl.ds(0, 16)], halo_next, 4 + 5, me)

    @pl.when(me < count - 1)
    def _():
        halo_out.start()

    @pl.when(me > 0)
    def _():
        next_out.start()

    own1 = scatter(snd1, rcv1, 0)
    own2 = [scatter(snd2.at[k], rcv2.at[k], sem) for k, sem in enumerate(LATER)]

    sums[...] = jnp.zeros_like(sums)
    grid[:, pl.ds(0, 8), :] = jnp.zeros((5, 8, TILE), F32)
    pgrad_rows[:, pl.ds(count, 8), :] = jnp.zeros((CHANS, 8, TILE), F32)
    ext[:, pl.ds(8, TILE), :] = st[...].astype(F32)

    @pl.when(me > 0)
    def _():
        halo_in.wait_recv()
        ext[:, pl.ds(0, 8), :] = halo[...].astype(F32)[:, 8:, :]

    @pl.when(me == 0)
    def _():
        ext[:, pl.ds(0, 8), :] = jnp.zeros((3, 8, ext.shape[2]), F32)

    @pl.when(me < count - 1)
    def _():
        next_in.wait_recv()
        ext[pl.ds(1, 2), pl.ds(8 + TILE, 8), :] = halo_next[...].astype(F32)[:, :8, :]

    @pl.when(me == count - 1)
    def _():
        ext[pl.ds(1, 2), pl.ds(8 + TILE, 8), :] = jnp.zeros((2, 8, width), F32)

    for i in range(3):
        number = TILE + 8 if i else TILE
        for q in range(width // TILE):
            lanes = pl.ds(q * TILE, TILE)
            total = None
            for j in range(reach + 1):
                term = taps[i, pl.ds(j, 1), lanes] * ext[i, pl.ds(8 - j, number), lanes]
                total = term if total is None else total + term
            local_qkv[i, pl.ds(0, number), lanes] = total

    def slot(index, c):
        if index in (1, 2, 3):
            return index, c
        return (0, 4)[c // 2], c % 2 + (2 if index == 4 else 0)

    def unpack(source, index):
        grid[index, pl.ds(8, count * CHANS), :] = source[...].astype(F32).reshape(count * CHANS, TILE)

    def plane(index, c):
        block, line = slot(index, c)
        return grid[block, pl.ds(8 + line, count, stride=CHANS), :]

    def convolve(index, c):
        here = plane(index, c)
        block, line = slot(index, c)
        before = grid[block, pl.ds(8 - CHANS + line, count, stride=CHANS), :]
        total = own_taps[c, index, pl.ds(0, 1), :] * here
        for j in range(1, reach + 1):
            moved = pltpu.roll(jnp.where(lane >= TILE - j, before, here), j, 1)
            shifts[index, c, j] = moved
            total = total + own_taps[c, index, pl.ds(j, 1), :] * moved
        qkv[index, c] = total
        return total

    def forward(planes, index, h):
        x = jnp.concatenate(planes, 1)
        y = dot(e1[...], jnp.concatenate([x, x], 0))
        re, im = y[:count], y[count:]
        twr, twi = tw[0], tw[1]
        tre, tim = re * twr - im * twi, re * twi + im * twr
        turned = jnp.concatenate(
            [jnp.concatenate([v[:, n * TILE : (n + 1) * TILE] for v in (tre, tim)], 1) for n in range(2)], 0
        )
        high, low = split(turned)
        spec[index, h] = dot(high, e2[0]) + dot(low, e2[0]) + dot(high, e2[1])

    def spectrum(index, h):
        return spec[index, h, :, pl.ds(0, TILE)], spec[index, h, :, pl.ds(TILE, TILE)]

    def inverse(re, im):
        high, low = split(jnp.concatenate([re, im], 1))
        u = dot(high, e2t[0]) + dot(low, e2t[0]) + dot(high, e2t[1])
        ur = jnp.concatenate([u[:count, :TILE], u[count:, :TILE]], 1)
        ui = jnp.concatenate([u[:count, TILE:], u[count:, TILE:]], 1)
        twr, twi = tw[0], tw[1]
        high, low = split(jnp.concatenate([ur * twr + ui * twi, ui * twr - ur * twi], 0))
        return dot(back[0], high) + dot(back[1], high) + dot(back[0], low)

    def put_rows(h, values):
        for n in range(2):
            rows[pl.ds(2 * h + n, count, stride=CHANS), :] = values[:, n * TILE : (n + 1) * TILE]

    def pack(which):
        ret_snd[which] = rows[...].astype(BF16).reshape(count, CHANS, TILE)

    def tap_sums(index, c, grad):
        for j in range(reach + 1):
            moved = plane(index, c) if j == 0 else shifts[index, c, j]
            part = jnp.sum((grad * moved).reshape(count // 8, 8, TILE), 0)
            sums[c * ENTRIES + index * (reach + 1) + j] = part

    own1.wait()
    others(snd1, rcv1, 0).wait_recv()
    unpack(rcv1.at[:, 0], 1)
    unpack(rcv1.at[:, 1], 2)
    for h in range(2):
        products = [(convolve(1, c) * convolve(2, c)).astype(BF16) for c in (2 * h, 2 * h + 1)]
        forward(products, 0, h)
    own2[0].wait()
    others(snd2.at[0], rcv2.at[0], LATER[0]).wait_recv()
    unpack(rcv2.at[0], 3)
    for h in range(2):
        forward([plane(3, c).astype(BF16) for c in (2 * h, 2 * h + 1)], 1, h)
        pr, pi = spectrum(0, h)
        fr, fi = spectrum(1, h)
        put_rows(h, inverse(pr * fr - pi * fi, pr * fi + pi * fr))
    pack(0)
    own3 = scatter(ret_snd.at[0], ret_rcv.at[0], 2)

    for c in range(CHANS):
        mixed_rows[c] = rows[pl.ds(c, count, stride=CHANS), :].astype(BF16).astype(F32)
    own4 = []
    for h in range(2):
        pair = (2 * h, 2 * h + 1)
        own2[1 + h].wait()
        others(snd2.at[1 + h], rcv2.at[1 + h], LATER[1 + h]).wait_recv()
        unpack(rcv2.at[1 + h], (0, 4)[h])
        forward([(plane(4, c) * convolve(0, c)).astype(BF16) for c in pair], 2, h)
        pr, pi = spectrum(0, h)
        fr, fi = spectrum(1, h)
        gr, gi = spectrum(2, h)
        pgrad = inverse(fr * gr + fi * gi, fr * gi - fi * gr)
        put_rows(0, pgrad)
        put_rows(1, inverse(pr * gr + pi * gi, pr * gi - pi * gr) * scale)
        pack(1 + h)
        own4.append(scatter(ret_snd.at[1 + h], ret_rcv.at[1 + h], 3 + h))
        for n, c in enumerate(pair):
            pgrad_rows[c, pl.ds(0, count), :] = pgrad[:, n * TILE : (n + 1) * TILE].astype(BF16).astype(F32)
    ahead = None
    for c in range(CHANS):
        tap_sums(0, c, plane(4, c) * mixed_rows[c])
        tap_sums(1, c, pgrad_rows[c, pl.ds(0, count), :] * qkv[2, c])
        tap_sums(2, c, pgrad_rows[c, pl.ds(0, count), :] * qkv[1, c])
        place = c * ENTRIES + AHEAD
        moved = pltpu.roll(pgrad_rows[c, pl.ds(1, count), :], place, 1)
        moved = jnp.where((lane >= place) & (lane < place + reach), moved, 0.0)
        ahead = moved if ahead is None else ahead + moved
    entries = jnp.sum(sums[...], 1)
    row = lax.dot_general(
        jnp.ones((8, TILE), F32), entries, (((1,), (1,)), ((), ())),
        precision=lax.Precision.HIGHEST, preferred_element_type=F32,
    )
    small[...] = (row[0:1] * scale + ahead).reshape(count, 1, TILE)
    own6 = scatter(small, tall, 5)

    strips = [pl.ds(q * TILE, TILE) for q in range(width // TILE)]

    edge, beyond = cgrad.at[0, pl.ds(0, 8)], cgrad.at[0, pl.ds(TILE, 8)]
    edge_out = remote(edge, beyond, 7, lax.rem(me + count - 1, count))
    edge_in = remote(edge, beyond, 7, me)

    def correlate(streams, first, number):
        for i in streams:
            for lanes in strips:
                total = None
                for j in range(reach + 1):
                    term = taps[i, pl.ds(j, 1), lanes] * cgrad[i, pl.ds(first + j, number), lanes]
                    total = term if total is None else total + term
                sgrad_ref[i, pl.ds(first, number), lanes] = total.astype(BF16)

    @pl.when(me == count - 1)
    def _():
        cgrad[0, pl.ds(TILE, 8), :] = jnp.zeros((8, width), F32)

    own3.wait()
    others(ret_snd.at[0], ret_rcv.at[0], 2).wait_recv()
    for q, lanes in enumerate(strips):
        mixed = turn_back(ret_rcv.at[0], q)
        gated_ref[:, lanes] = (local_qkv[0, pl.ds(0, TILE), lanes] * mixed).astype(BF16)
        cgrad[0, pl.ds(0, TILE), lanes] = ct[:, lanes].astype(F32) * mixed

    @pl.when(me > 0)
    def _():
        edge_out.start()

    correlate((0,), 0, TILE - 16)
    for h in range(2):
        own4[h].wait()
        others(ret_snd.at[1 + h], ret_rcv.at[1 + h], 3 + h).wait_recv()
    for q, lanes in enumerate(strips):
        pgrad = jnp.where(low, turn_back(ret_rcv.at[1], q), pltpu.roll(turn_back(ret_rcv.at[2], q), 2, 1))
        cgrad[1, pl.ds(0, TILE), lanes] = pgrad * local_qkv[2, pl.ds(0, TILE), lanes]
        cgrad[2, pl.ds(0, TILE), lanes] = pgrad * local_qkv[1, pl.ds(0, TILE), lanes]
    for q, lanes in enumerate(strips):
        fgrad = jnp.where(low, pltpu.roll(turn_back(ret_rcv.at[1], q), TILE - 2, 1), turn_back(ret_rcv.at[2], q))
        fgrad_ref[:, lanes] = fgrad.astype(BF16)
    correlate((1, 2), 0, TILE - 16)

    @pl.when(me < count - 1)
    def _():
        edge_in.wait_recv()

    correlate((0,), TILE - 16, 16)
    own6.wait()
    others(small, tall, 5).wait_recv()
    shared = tall[...].reshape(count, TILE)
    for c in range(CHANS):
        moved = pltpu.roll(shared, TILE - c * ENTRIES, 1) if c else shared
        spread[pl.ds(c, count, stride=CHANS), :] = moved
    terms = reach + 1
    for q, lanes in enumerate(strips):
        by_entry = spread[pl.ds(q * TILE, TILE), :].T
        for i in range(3):
            tgrad_ref[i, :, lanes] = by_entry[i * terms : (i + 1) * terms]
        following = by_entry[AHEAD : AHEAD + 8]
        cgrad[1, pl.ds(TILE, 8), lanes] = following * local_qkv[2, pl.ds(TILE, 8), lanes]
        cgrad[2, pl.ds(TILE, 8), lanes] = following * local_qkv[1, pl.ds(TILE, 8), lanes]
    correlate((1, 2), TILE - 16, 16)
    others(snd1, rcv1, 0).wait_send()
    for k, sem in enumerate(LATER):
        others(snd2.at[k], rcv2.at[k], sem).wait_send()
    for k in range(3):
        others(ret_snd.at[k], ret_rcv.at[k], 2 + k).wait_send()
    others(small, tall, 5).wait_send()

    @pl.when(me < count - 1)
    def _():
        halo_out.wait_send()

    @pl.when(me > 0)
    def _():
        next_out.wait_send()
        edge_out.wait_send()


def result_kernel(*refs):
    number = len(refs) // 2
    sem = refs[-1]
    stores = [
        pltpu.make_async_copy(source, target, sem.at[i])
        for i, (source, target) in enumerate(zip(refs[:number], refs[number : 2 * number]))
    ]
    for store in stores:
        store.start()
    for store in stores:
        store.wait()


def local(streams, taps, filters, cotangent):
    rows, width = filters.shape
    count = lax.axis_size("ctx")
    assert rows == TILE and width == CHANS * count and count == TILE == Y_SIZE * Z_SIZE * X_SIZE
    tables = [jnp.asarray(t) for t in make_tables(count, rows)]
    reach = taps.shape[1] - 1
    hbm = pl.BlockSpec(memory_space=pltpu.HBM)
    vmem = pl.BlockSpec(memory_space=VMEM)
    line = (count, CHANS, TILE)
    pair = (count, 2, CHANS, TILE)
    scratch = [
        VMEM(streams.shape, BF16), VMEM(filters.shape, BF16), VMEM(cotangent.shape, BF16), VMEM(taps.shape, F32),
        *[VMEM(t.shape, t.dtype) for t in tables],
        VMEM(pair, BF16), VMEM((3,) + line, BF16), VMEM(pair, BF16), VMEM((3,) + line, BF16),
        VMEM((CHANS, 3, 8, TILE), F32),
        VMEM((5, 8 + count * CHANS, TILE), F32),
        VMEM((3, CHANS, reach + 1, count, TILE), F32),
        VMEM((3, CHANS, count, TILE), F32),
        VMEM((3, 2, 2 * count, 2 * TILE), F32),
        VMEM((count * CHANS, TILE), F32), VMEM((CHANS, count, TILE), F32), VMEM((CHANS, count + 8, TILE), F32),
        VMEM((3,) + line, BF16), VMEM((3,) + line, BF16),
        VMEM((TILE, 8, TILE), F32), VMEM((count, 1, TILE), F32), VMEM((count, 1, TILE), F32),
        VMEM((count * CHANS, TILE), F32),
        VMEM((3, 16, width), BF16), VMEM((2, 16, width), BF16),
        VMEM((3, 8 + TILE + 8, width), F32),
        VMEM((3, TILE + 8, width), F32),
        VMEM((3, TILE + 8, width), F32),
        pltpu.SemaphoreType.DMA((9,)), pltpu.SemaphoreType.DMA((11,)),
        pltpu.SemaphoreType.DMA((11,)), pltpu.SemaphoreType.DMA((11,)),
    ]
    parts = pl.pallas_call(
        block_kernel,
        out_shape=[
            jax.ShapeDtypeStruct(cotangent.shape, BF16),
            jax.ShapeDtypeStruct(streams.shape, BF16),
            jax.ShapeDtypeStruct(filters.shape, BF16),
            jax.ShapeDtypeStruct(taps.shape, F32),
        ],
        in_specs=[hbm] * 9,
        out_specs=[vmem] * 4,
        scratch_shapes=scratch,
        compiler_params=pltpu.CompilerParams(
            collective_id=0, has_side_effects=True, vmem_limit_bytes=40 << 20
        ),
    )(*[pltpu.with_memory_space_constraint(x, pltpu.HBM) for x in (streams, filters, cotangent, taps, *tables)])
    return pl.pallas_call(
        result_kernel,
        out_shape=[
            jax.ShapeDtypeStruct(cotangent.shape, BF16),
            jax.ShapeDtypeStruct(streams.shape, BF16),
            jax.ShapeDtypeStruct(filters.shape, BF16),
            jax.ShapeDtypeStruct(taps.shape, F32),
        ],
        in_specs=[vmem] * 4,
        out_specs=[hbm] * 4,
        scratch_shapes=[pltpu.SemaphoreType.DMA((4,))],
        compiler_params=pltpu.CompilerParams(vmem_limit_bytes=8 << 20),
    )(*parts)


def solution(mesh):
    in_specs = (P(None, "ctx", "fft"), P(None, None, "fft"), P("ctx", "fft"), P("ctx", "fft"))
    out_specs = (P("ctx", "fft"), P(None, "ctx", "fft"), P("ctx", "fft"), P(None, None, "fft"))
    return jax.shard_map(local, mesh=mesh, in_specs=in_specs, out_specs=out_specs, check_vma=False)
```

```python
import math

import jax
import jax.numpy as jnp
import numpy as np
from jax import lax
from jax.experimental import pallas as pl
from jax.experimental.pallas import tpu as pltpu
from jax.sharding import PartitionSpec as P

MESH = pl.DeviceIdType.MESH
VMEM = pltpu.VMEM
F32 = jnp.float32
BF16 = jnp.bfloat16
CHANS = 4
TILE = 128
ENTRIES = 32
AHEAD = 24
Y_SIZE, Z_SIZE, X_SIZE = 8, 8, 2
LATER = (1, 8, 10)


def halves(table):
    high = table.astype(BF16)
    return high, (table - high.astype(np.float64)).astype(BF16)


def make_tables(a_size, b_size):
    k1, a, b, k2 = (np.arange(n, dtype=np.int64) for n in (a_size, a_size, b_size, b_size))
    first = (4 * k1[:, None] + 1) * a[None, :] % (4 * a_size) / (4.0 * a_size)
    twist = (4 * k1[:, None] + 1) * b[None, :] % (4 * a_size * b_size) / (4.0 * a_size * b_size)
    second = b[:, None] * k2[None, :] % b_size / float(b_size)
    first, twist, second = (np.exp(-2j * np.pi * x) for x in (first, twist, second))
    e1 = np.concatenate([first.real, first.imag], 0)
    e2 = np.block([[second.real, second.imag], [-second.imag, second.real]])
    back = np.concatenate([first.real.T, first.imag.T], 1) / (a_size * b_size)
    e1 = np.concatenate(halves(e1), 1)
    e2, e2t, back = (np.stack(halves(x)) for x in (e2, e2.T, back))
    twist = np.stack([np.tile(x, (1, 2)) for x in (twist.real, twist.imag)]).astype(np.float32)
    stacked = np.concatenate([x.reshape(-1, 2 * b_size) for x in (e1, e2, e2t, back)], 0)
    return stacked, twist


def dot(a, b):
    return jnp.dot(a, b, preferred_element_type=F32)


def split(x):
    high = x.astype(BF16)
    return high, (x - high.astype(F32)).astype(BF16)


def turn_back(source, q):
    tile = source[pl.ds(q * TILE // CHANS, TILE // CHANS)].astype(F32).reshape(TILE, TILE)
    return tile.T


def block_kernel(
    streams_hbm, filters_hbm, cot_hbm, taps_hbm, dft_hbm, tw_hbm,
    gated_ref, sgrad_ref, fgrad_ref, tgrad_ref,
    st, fl, ct, taps, dft, tw,
    snd1, snd2, rcv1, rcv2, own_taps, grid, shifts, qkv, spec, rows, mixed_rows, pgrad_rows, ret_snd, ret_rcv,
    sums, small, tall, spread, halo, halo_next, ext, local_qkv, cgrad,
    in_sem, send_sem, recv_sem,
):
    count = rcv1.shape[0]
    width = ext.shape[2]
    reach = taps.shape[1] - 1
    scale = 1.0 / math.sqrt(count * TILE)
    me = lax.axis_index("ctx")
    barrier = pltpu.get_barrier_semaphore()

    def remote(source, target, sem, peer):
        return pltpu.make_async_remote_copy(
            source, target, send_sem.at[sem], recv_sem.at[sem], device_id={"ctx": peer}, device_id_type=MESH
        )

    zx_count = Z_SIZE * X_SIZE
    y, zx = me // zx_count, lax.rem(me, zx_count)
    z, x = zx // X_SIZE, lax.rem(zx, X_SIZE)
    planes = [
        lax.rem(z + dz, Z_SIZE) * X_SIZE + lax.rem(x + dx, X_SIZE)
        for dz in (4, 3, 5, 2, 6, 1, 7, 0)
        for dx in (1, 0)
    ]

    def each_peer(visit):
        def row(step, carry):
            half = (step + 1) // 2
            dy = 4 + half - 2 * half * lax.rem(step, 2)
            base = lax.rem(y + dy, Y_SIZE) * zx_count
            for plane_at in planes:
                visit(base + plane_at)
            return carry

        lax.fori_loop(0, Y_SIZE - 1, row, 0)
        for plane_at in planes[:-1]:
            visit(y * zx_count + plane_at)

    loads = [
        pltpu.make_async_copy(source, target, in_sem.at[i])
        for i, (source, target) in enumerate(
            (
                (streams_hbm, st), (filters_hbm, fl), (cot_hbm, ct), (taps_hbm, taps), (dft_hbm, dft),
                (tw_hbm, tw),
            )
        )
    ]
    for load in loads:
        load.start()

    def greet(peer):
        pl.semaphore_signal(barrier, inc=1, device_id={"ctx": peer}, device_id_type=MESH)

    each_peer(greet)

    def turn_out(source, target):
        for q in range(source.shape[1] // TILE):
            tile = source[:, q * TILE : (q + 1) * TILE].astype(F32).T
            target[pl.ds(q * TILE // CHANS, TILE // CHANS)] = tile.astype(BF16).reshape(-1, CHANS, TILE)

    loads[0].wait()
    turn_out(st.at[1], snd1.at[:, 0])
    turn_out(st.at[2], snd1.at[:, 1])
    loads[1].wait()
    turn_out(fl, snd2.at[0])
    loads[2].wait()
    lane = lax.broadcasted_iota(jnp.int32, (TILE, TILE), 1)
    low = lax.rem(lane, CHANS) < 2
    for q in range(width // TILE):
        lanes = pl.ds(q * TILE, TILE)
        place = pl.ds(q * TILE // CHANS, TILE // CHANS)
        first, second = st[0, :, lanes].astype(F32), ct[:, lanes].astype(F32)
        tiles = (
            jnp.where(low, first, pltpu.roll(second, 2, 1)),
            jnp.where(low, pltpu.roll(first, TILE - 2, 1), second),
        )
        for h, tile in enumerate(tiles):
            snd2.at[1 + h][place] = tile.T.astype(BF16).reshape(-1, CHANS, TILE)
    for load in loads[3:]:
        load.wait()
    for i in range(3):
        for c in range(CHANS):
            chosen = lax.broadcasted_iota(jnp.int32, (reach + 1, width), 1) == CHANS * me + c
            tap = jnp.sum(jnp.where(chosen, taps[i], 0.0), 1, keepdims=True)
            own_taps[c, i, pl.ds(0, reach + 1), :] = jnp.broadcast_to(tap, (reach + 1, TILE))

    def scatter(source, target, sem):
        each_peer(lambda peer: remote(source.at[peer], target.at[me], sem, peer).start())
        target[me] = source[me]

    def others(source, target, sem):
        return remote(source.at[pl.ds(0, count - 1)], target.at[pl.ds(0, count - 1)], sem, me)

    pl.semaphore_wait(barrier, count - 1)
    halo_out = remote(st.at[:, pl.ds(TILE - 16, 16)], halo, 6, lax.rem(me + 1, count))
    halo_in = remote(st.at[:, pl.ds(TILE - 16, 16)], halo, 6, me)

    next_out = remote(st.at[pl.ds(1, 2), pl.ds(0, 16)], halo_next, 4 + 5, lax.rem(me + count - 1, count))
    next_in = remote(st.at[pl.ds(1, 2), pl.ds(0, 16)], halo_next, 4 + 5, me)

    @pl.when(me < count - 1)
    def _():
        halo_out.start()

    @pl.when(me > 0)
    def _():
        next_out.start()

    scatter(snd1, rcv1, 0)
    for k, sem in enumerate(LATER):
        scatter(snd2.at[k], rcv2.at[k], sem)

    sums[...] = jnp.zeros_like(sums)
    grid[:, pl.ds(0, 8), :] = jnp.zeros((5, 8, TILE), F32)
    pgrad_rows[:, pl.ds(count, 8), :] = jnp.zeros((CHANS, 8, TILE), F32)
    ext[:, pl.ds(8, TILE), :] = st[...].astype(F32)

    @pl.when(me > 0)
    def _():
        halo_in.wait_recv()
        ext[:, pl.ds(0, 8), :] = halo[...].astype(F32)[:, 8:, :]

    @pl.when(me == 0)
    def _():
        ext[:, pl.ds(0, 8), :] = jnp.zeros((3, 8, ext.shape[2]), F32)

    @pl.when(me < count - 1)
    def _():
        next_in.wait_recv()
        ext[pl.ds(1, 2), pl.ds(8 + TILE, 8), :] = halo_next[...].astype(F32)[:, :8, :]

    @pl.when(me == count - 1)
    def _():
        ext[pl.ds(1, 2), pl.ds(8 + TILE, 8), :] = jnp.zeros((2, 8, width), F32)

    for i in range(3):
        number = TILE + 8 if i else TILE
        for q in range(width // TILE):
            lanes = pl.ds(q * TILE, TILE)
            total = None
            for j in range(reach + 1):
                term = taps[i, pl.ds(j, 1), lanes] * ext[i, pl.ds(8 - j, number), lanes]
                total = term if total is None else total + term
            local_qkv[i, pl.ds(0, number), lanes] = total

    def slot(index, c):
        if index in (1, 2, 3):
            return index, c
        return (0, 4)[c // 2], c % 2 + (2 if index == 4 else 0)

    def unpack(source, index):
        grid[index, pl.ds(8, count * CHANS), :] = source[...].astype(F32).reshape(count * CHANS, TILE)

    def plane(index, c):
        block, line = slot(index, c)
        return grid[block, pl.ds(8 + line, count, stride=CHANS), :]

    def convolve(index, c):
        here = plane(index, c)
        block, line = slot(index, c)
        before = grid[block, pl.ds(8 - CHANS + line, count, stride=CHANS), :]
        total = own_taps[c, index, pl.ds(0, 1), :] * here
        for j in range(1, reach + 1):
            moved = pltpu.roll(jnp.where(lane >= TILE - j, before, here), j, 1)
            shifts[index, c, j] = moved
            total = total + own_taps[c, index, pl.ds(j, 1), :] * moved
        qkv[index, c] = total
        return total

    size = 2 * TILE
    e1 = dft.at[pl.ds(0, size)]
    e2 = [dft.at[pl.ds((1 + k) * size, size)] for k in range(2)]
    e2t = [dft.at[pl.ds((3 + k) * size, size)] for k in range(2)]
    back = [dft.at[pl.ds(5 * size + k * TILE, TILE)] for k in range(2)]

    def forward(planes, index, h):
        x = jnp.concatenate(planes, 1)
        y = dot(e1[...], jnp.concatenate([x, x], 0))
        re, im = y[:count], y[count:]
        twr, twi = tw[0], tw[1]
        tre, tim = re * twr - im * twi, re * twi + im * twr
        turned = jnp.concatenate(
            [jnp.concatenate([v[:, n * TILE : (n + 1) * TILE] for v in (tre, tim)], 1) for n in range(2)], 0
        )
        high, low = split(turned)
        spec[index, h] = dot(high, e2[0][...]) + dot(low, e2[0][...]) + dot(high, e2[1][...])

    def spectrum(index, h):
        return spec[index, h, :, pl.ds(0, TILE)], spec[index, h, :, pl.ds(TILE, TILE)]

    def inverse(re, im):
        high, low = split(jnp.concatenate([re, im], 1))
        u = dot(high, e2t[0][...]) + dot(low, e2t[0][...]) + dot(high, e2t[1][...])
        ur = jnp.concatenate([u[:count, :TILE], u[count:, :TILE]], 1)
        ui = jnp.concatenate([u[:count, TILE:], u[count:, TILE:]], 1)
        twr, twi = tw[0], tw[1]
        high, low = split(jnp.concatenate([ur * twr + ui * twi, ui * twr - ur * twi], 0))
        return dot(back[0][...], high) + dot(back[1][...], high) + dot(back[0][...], low)

    def put_rows(h, values):
        for n in range(2):
            rows[pl.ds(2 * h + n, count, stride=CHANS), :] = values[:, n * TILE : (n + 1) * TILE]

    def pack(which):
        ret_snd[which] = rows[...].astype(BF16).reshape(count, CHANS, TILE)

    def tap_sums(index, c, grad):
        for j in range(reach + 1):
            moved = plane(index, c) if j == 0 else shifts[index, c, j]
            part = jnp.sum((grad * moved).reshape(count // 8, 8, TILE), 0)
            sums[c * ENTRIES + index * (reach + 1) + j] = part

    others(snd1, rcv1, 0).wait_recv()
    unpack(rcv1.at[:, 0], 1)
    unpack(rcv1.at[:, 1], 2)
    for h in range(2):
        products = [(convolve(1, c) * convolve(2, c)).astype(BF16) for c in (2 * h, 2 * h + 1)]
        forward(products, 0, h)
    others(snd2.at[0], rcv2.at[0], LATER[0]).wait_recv()
    unpack(rcv2.at[0], 3)
    for h in range(2):
        forward([plane(3, c).astype(BF16) for c in (2 * h, 2 * h + 1)], 1, h)
        pr, pi = spectrum(0, h)
        fr, fi = spectrum(1, h)
        put_rows(h, inverse(pr * fr - pi * fi, pr * fi + pi * fr))
    pack(0)
    scatter(ret_snd.at[0], ret_rcv.at[0], 2)

    for c in range(CHANS):
        mixed_rows[c] = rows[pl.ds(c, count, stride=CHANS), :].astype(BF16).astype(F32)
    for h in range(2):
        pair = (2 * h, 2 * h + 1)
        others(snd2.at[1 + h], rcv2.at[1 + h], LATER[1 + h]).wait_recv()
        unpack(rcv2.at[1 + h], (0, 4)[h])
        forward([(plane(4, c) * convolve(0, c)).astype(BF16) for c in pair], 2, h)
        pr, pi = spectrum(0, h)
        fr, fi = spectrum(1, h)
        gr, gi = spectrum(2, h)
        pgrad = inverse(fr * gr + fi * gi, fr * gi - fi * gr)
        put_rows(0, pgrad)
        put_rows(1, inverse(pr * gr + pi * gi, pr * gi - pi * gr) * scale)
        pack(1 + h)
        scatter(ret_snd.at[1 + h], ret_rcv.at[1 + h], 3 + h)
        for n, c in enumerate(pair):
            pgrad_rows[c, pl.ds(0, count), :] = pgrad[:, n * TILE : (n + 1) * TILE].astype(BF16).astype(F32)
    ahead = None
    for c in range(CHANS):
        tap_sums(0, c, plane(4, c) * mixed_rows[c])
        tap_sums(1, c, pgrad_rows[c, pl.ds(0, count), :] * qkv[2, c])
        tap_sums(2, c, pgrad_rows[c, pl.ds(0, count), :] * qkv[1, c])
        place = c * ENTRIES + AHEAD
        moved = pltpu.roll(pgrad_rows[c, pl.ds(1, count), :], place, 1)
        moved = jnp.where((lane >= place) & (lane < place + reach), moved, 0.0)
        ahead = moved if ahead is None else ahead + moved
    entries = jnp.sum(sums[...], 1)
    row = lax.dot_general(
        jnp.ones((8, TILE), F32), entries, (((1,), (1,)), ((), ())),
        precision=lax.Precision.HIGHEST, preferred_element_type=F32,
    )
    small[...] = (row[0:1] * scale + ahead).reshape(count, 1, TILE)
    scatter(small, tall, 5)

    strips = [pl.ds(q * TILE, TILE) for q in range(width // TILE)]

    edge, beyond = cgrad.at[0, pl.ds(0, 8)], cgrad.at[0, pl.ds(TILE, 8)]
    edge_out = remote(edge, beyond, 7, lax.rem(me + count - 1, count))
    edge_in = remote(edge, beyond, 7, me)

    def correlate(streams, first, number):
        for i in streams:
            for lanes in strips:
                total = None
                for j in range(reach + 1):
                    term = taps[i, pl.ds(j, 1), lanes] * cgrad[i, pl.ds(first + j, number), lanes]
                    total = term if total is None else total + term
                sgrad_ref[i, pl.ds(first, number), lanes] = total.astype(BF16)

    @pl.when(me == count - 1)
    def _():
        cgrad[0, pl.ds(TILE, 8), :] = jnp.zeros((8, width), F32)

    others(ret_snd.at[0], ret_rcv.at[0], 2).wait_recv()
    for q, lanes in enumerate(strips):
        mixed = turn_back(ret_rcv.at[0], q)
        gated_ref[:, lanes] = (local_qkv[0, pl.ds(0, TILE), lanes] * mixed).astype(BF16)
        cgrad[0, pl.ds(0, TILE), lanes] = ct[:, lanes].astype(F32) * mixed

    @pl.when(me > 0)
    def _():
        edge_out.start()

    correlate((0,), 0, TILE - 16)
    for h in range(2):
        others(ret_snd.at[1 + h], ret_rcv.at[1 + h], 3 + h).wait_recv()
    for q, lanes in enumerate(strips):
        pgrad = jnp.where(low, turn_back(ret_rcv.at[1], q), pltpu.roll(turn_back(ret_rcv.at[2], q), 2, 1))
        cgrad[1, pl.ds(0, TILE), lanes] = pgrad * local_qkv[2, pl.ds(0, TILE), lanes]
        cgrad[2, pl.ds(0, TILE), lanes] = pgrad * local_qkv[1, pl.ds(0, TILE), lanes]
    for q, lanes in enumerate(strips):
        fgrad = jnp.where(low, pltpu.roll(turn_back(ret_rcv.at[1], q), TILE - 2, 1), turn_back(ret_rcv.at[2], q))
        fgrad_ref[:, lanes] = fgrad.astype(BF16)
    correlate((1, 2), 0, TILE - 16)

    @pl.when(me < count - 1)
    def _():
        edge_in.wait_recv()

    correlate((0,), TILE - 16, 16)
    others(small, tall, 5).wait_recv()
    shared = tall[...].reshape(count, TILE)
    for c in range(CHANS):
        moved = pltpu.roll(shared, TILE - c * ENTRIES, 1) if c else shared
        spread[pl.ds(c, count, stride=CHANS), :] = moved
    terms = reach + 1
    for q, lanes in enumerate(strips):
        by_entry = spread[pl.ds(q * TILE, TILE), :].T
        for i in range(3):
            tgrad_ref[i, :, lanes] = by_entry[i * terms : (i + 1) * terms]
        following = by_entry[AHEAD : AHEAD + 8]
        cgrad[1, pl.ds(TILE, 8), lanes] = following * local_qkv[2, pl.ds(TILE, 8), lanes]
        cgrad[2, pl.ds(TILE, 8), lanes] = following * local_qkv[1, pl.ds(TILE, 8), lanes]
    correlate((1, 2), TILE - 16, 16)
    others(snd1, rcv1, 0).wait_send()
    for k, sem in enumerate(LATER):
        others(snd2.at[k], rcv2.at[k], sem).wait_send()
    for k in range(3):
        others(ret_snd.at[k], ret_rcv.at[k], 2 + k).wait_send()
    others(small, tall, 5).wait_send()

    @pl.when(me < count - 1)
    def _():
        halo_out.wait_send()

    @pl.when(me > 0)
    def _():
        next_out.wait_send()
        edge_out.wait_send()


def result_kernel(*refs):
    number = len(refs) // 2
    sem = refs[-1]
    stores = [
        pltpu.make_async_copy(source, target, sem.at[i])
        for i, (source, target) in enumerate(zip(refs[:number], refs[number : 2 * number]))
    ]
    for store in stores:
        store.start()
    for store in stores:
        store.wait()


def local(streams, taps, filters, cotangent):
    rows, width = filters.shape
    count = lax.axis_size("ctx")
    assert rows == TILE and width == CHANS * count and count == TILE == Y_SIZE * Z_SIZE * X_SIZE
    tables = [jnp.asarray(t) for t in make_tables(count, rows)]
    reach = taps.shape[1] - 1
    hbm = pl.BlockSpec(memory_space=pltpu.HBM)
    vmem = pl.BlockSpec(memory_space=VMEM)
    line = (count, CHANS, TILE)
    pair = (count, 2, CHANS, TILE)
    scratch = [
        VMEM(streams.shape, BF16), VMEM(filters.shape, BF16), VMEM(cotangent.shape, BF16), VMEM(taps.shape, F32),
        *[VMEM(t.shape, t.dtype) for t in tables],
        VMEM(pair, BF16), VMEM((3,) + line, BF16), VMEM(pair, BF16), VMEM((3,) + line, BF16),
        VMEM((CHANS, 3, 8, TILE), F32),
        VMEM((5, 8 + count * CHANS, TILE), F32),
        VMEM((3, CHANS, reach + 1, count, TILE), F32),
        VMEM((3, CHANS, count, TILE), F32),
        VMEM((3, 2, 2 * count, 2 * TILE), F32),
        VMEM((count * CHANS, TILE), F32), VMEM((CHANS, count, TILE), F32), VMEM((CHANS, count + 8, TILE), F32),
        VMEM((3,) + line, BF16), VMEM((3,) + line, BF16),
        VMEM((TILE, 8, TILE), F32), VMEM((count, 1, TILE), F32), VMEM((count, 1, TILE), F32),
        VMEM((count * CHANS, TILE), F32),
        VMEM((3, 16, width), BF16), VMEM((2, 16, width), BF16),
        VMEM((3, 8 + TILE + 8, width), F32),
        VMEM((3, TILE + 8, width), F32),
        VMEM((3, TILE + 8, width), F32),
        pltpu.SemaphoreType.DMA((6,)), pltpu.SemaphoreType.DMA((11,)), pltpu.SemaphoreType.DMA((11,)),
    ]
    parts = pl.pallas_call(
        block_kernel,
        out_shape=[
            jax.ShapeDtypeStruct(cotangent.shape, BF16),
            jax.ShapeDtypeStruct(streams.shape, BF16),
            jax.ShapeDtypeStruct(filters.shape, BF16),
            jax.ShapeDtypeStruct(taps.shape, F32),
        ],
        in_specs=[hbm] * 6,
        out_specs=[vmem] * 4,
        scratch_shapes=scratch,
        compiler_params=pltpu.CompilerParams(
            collective_id=0, has_side_effects=True, vmem_limit_bytes=40 << 20
        ),
    )(*[pltpu.with_memory_space_constraint(x, pltpu.HBM) for x in (streams, filters, cotangent, taps, *tables)])
    return pl.pallas_call(
        result_kernel,
        out_shape=[
            jax.ShapeDtypeStruct(cotangent.shape, BF16),
            jax.ShapeDtypeStruct(streams.shape, BF16),
            jax.ShapeDtypeStruct(filters.shape, BF16),
            jax.ShapeDtypeStruct(taps.shape, F32),
        ],
        in_specs=[vmem] * 4,
        out_specs=[hbm] * 4,
        scratch_shapes=[pltpu.SemaphoreType.DMA((4,))],
        compiler_params=pltpu.CompilerParams(vmem_limit_bytes=8 << 20),
    )(*parts)


def solution(mesh):
    in_specs = (P(None, "ctx", "fft"), P(None, None, "fft"), P("ctx", "fft"), P("ctx", "fft"))
    out_specs = (P("ctx", "fft"), P(None, "ctx", "fft"), P("ctx", "fft"), P(None, None, "fft"))
    return jax.shard_map(local, mesh=mesh, in_specs=in_specs, out_specs=out_specs, check_vma=False)
```

```python
import math

import jax
import jax.numpy as jnp
import numpy as np
from jax import lax
from jax.experimental import pallas as pl
from jax.experimental.pallas import tpu as pltpu
from jax.sharding import PartitionSpec as P

MESH = pl.DeviceIdType.MESH
VMEM = pltpu.VMEM
F32 = jnp.float32
BF16 = jnp.bfloat16
CHANS = 4
TILE = 128
ENTRIES = 32
AHEAD = 24
Y_SIZE, Z_SIZE, X_SIZE = 8, 8, 2
LATER = (1, 8, 10)


def halves(table):
    high = table.astype(BF16)
    return high, (table - high.astype(np.float64)).astype(BF16)


def make_tables(a_size, b_size):
    k1, a, b, k2 = (np.arange(n, dtype=np.int64) for n in (a_size, a_size, b_size, b_size))
    first = (4 * k1[:, None] + 1) * a[None, :] % (4 * a_size) / (4.0 * a_size)
    twist = (4 * k1[:, None] + 1) * b[None, :] % (4 * a_size * b_size) / (4.0 * a_size * b_size)
    second = b[:, None] * k2[None, :] % b_size / float(b_size)
    first, twist, second = (np.exp(-2j * np.pi * x) for x in (first, twist, second))
    e1 = np.concatenate([first.real, first.imag], 0)
    e2 = np.block([[second.real, second.imag], [-second.imag, second.real]])
    back = np.concatenate([first.real.T, first.imag.T], 1) / (a_size * b_size)
    e1 = np.concatenate(halves(e1), 1)
    e2, e2t, back = (np.stack(halves(x)) for x in (e2, e2.T, back))
    twist = np.stack([np.tile(x, (1, 2)) for x in (twist.real, twist.imag)]).astype(np.float32)
    stacked = np.concatenate([x.reshape(-1, 2 * b_size) for x in (e1, e2, e2t, back)], 0)
    return stacked, twist


def dot(a, b):
    return jnp.dot(a, b, preferred_element_type=F32)


def split(x):
    high = x.astype(BF16)
    return high, (x - high.astype(F32)).astype(BF16)


def turn_back(source, q):
    tile = source[pl.ds(q * TILE // CHANS, TILE // CHANS)].astype(F32).reshape(TILE, TILE)
    return tile.T


def block_kernel(
    streams_hbm, filters_hbm, cot_hbm, taps_hbm, dft_hbm, tw_hbm,
    gated_ref, sgrad_ref, fgrad_ref, tgrad_ref,
    st, fl, ct, taps, dft, tw,
    snd1, snd2, rcv1, rcv2, own_taps, grid, shifts, qkv, spec, rows, mixed_rows, pgrad_rows, ret_snd, ret_rcv,
    sums, small, tall, spread, halo, halo_next, ext, local_qkv, cgrad,
    in_sem, send_sem, recv_sem,
):
    count = rcv1.shape[0]
    width = ext.shape[2]
    reach = taps.shape[1] - 1
    scale = 1.0 / math.sqrt(count * TILE)
    me = lax.axis_index("ctx")
    barrier = pltpu.get_barrier_semaphore()

    def remote(source, target, sem, peer):
        return pltpu.make_async_remote_copy(
            source, target, send_sem.at[sem], recv_sem.at[sem], device_id={"ctx": peer}, device_id_type=MESH
        )

    zx_count = Z_SIZE * X_SIZE
    y, zx = me // zx_count, lax.rem(me, zx_count)
    z, x = zx // X_SIZE, lax.rem(zx, X_SIZE)
    planes = [
        lax.rem(z + dz, Z_SIZE) * X_SIZE + lax.rem(x + dx, X_SIZE)
        for dz in (4, 3, 5, 2, 6, 1, 7, 0)
        for dx in (1, 0)
    ]

    def each_peer(visit):
        def row(step, carry):
            half = (step + 1) // 2
            dy = 4 + half - 2 * half * lax.rem(step, 2)
            base = lax.rem(y + dy, Y_SIZE) * zx_count
            for plane_at in planes:
                visit(base + plane_at)
            return carry

        lax.fori_loop(0, Y_SIZE - 1, row, 0)
        for plane_at in planes[:-1]:
            visit(y * zx_count + plane_at)

    loads = [
        pltpu.make_async_copy(source, target, in_sem.at[i])
        for i, (source, target) in enumerate(
            (
                (streams_hbm, st), (filters_hbm, fl), (cot_hbm, ct), (taps_hbm, taps), (dft_hbm, dft),
                (tw_hbm, tw),
            )
        )
    ]
    for load in loads:
        load.start()

    def greet(peer):
        pl.semaphore_signal(barrier, inc=1, device_id={"ctx": peer}, device_id_type=MESH)

    each_peer(greet)

    def turn_out(source, target):
        for q in range(source.shape[1] // TILE):
            tile = source[:, q * TILE : (q + 1) * TILE].astype(F32).T
            target[pl.ds(q * TILE // CHANS, TILE // CHANS)] = tile.astype(BF16).reshape(-1, CHANS, TILE)

    loads[0].wait()
    turn_out(st.at[1], snd1.at[:, 0])
    turn_out(st.at[2], snd1.at[:, 1])
    loads[1].wait()
    turn_out(fl, snd2.at[0])
    loads[2].wait()
    lane = lax.broadcasted_iota(jnp.int32, (TILE, TILE), 1)
    low = lax.rem(lane, CHANS) < 2
    for q in range(width // TILE):
        lanes = pl.ds(q * TILE, TILE)
        place = pl.ds(q * TILE // CHANS, TILE // CHANS)
        first, second = st[0, :, lanes].astype(F32), ct[:, lanes].astype(F32)
        tiles = (
            jnp.where(low, first, pltpu.roll(second, 2, 1)),
            jnp.where(low, pltpu.roll(first, TILE - 2, 1), second),
        )
        for h, tile in enumerate(tiles):
            snd2.at[1 + h][place] = tile.T.astype(BF16).reshape(-1, CHANS, TILE)
    for load in loads[3:]:
        load.wait()
    for i in range(3):
        for c in range(CHANS):
            chosen = lax.broadcasted_iota(jnp.int32, (reach + 1, width), 1) == CHANS * me + c
            tap = jnp.sum(jnp.where(chosen, taps[i], 0.0), 1, keepdims=True)
            own_taps[c, i, pl.ds(0, reach + 1), :] = jnp.broadcast_to(tap, (reach + 1, TILE))

    def scatter(source, target, sem):
        each_peer(lambda peer: remote(source.at[peer], target.at[me], sem, peer).start())
        target[me] = source[me]

    def others(source, target, sem):
        return remote(source.at[pl.ds(0, count - 1)], target.at[pl.ds(0, count - 1)], sem, me)

    pl.semaphore_wait(barrier, count - 1)
    halo_out = remote(st.at[:, pl.ds(TILE - 8, 8)], halo, 6, lax.rem(me + 1, count))
    halo_in = remote(st.at[:, pl.ds(TILE - 8, 8)], halo, 6, me)

    next_out = remote(st.at[pl.ds(1, 2), pl.ds(0, 8)], halo_next, 4 + 5, lax.rem(me + count - 1, count))
    next_in = remote(st.at[pl.ds(1, 2), pl.ds(0, 8)], halo_next, 4 + 5, me)

    @pl.when(me < count - 1)
    def _():
        halo_out.start()

    @pl.when(me > 0)
    def _():
        next_out.start()

    scatter(snd1, rcv1, 0)
    for k, sem in enumerate(LATER):
        scatter(snd2.at[k], rcv2.at[k], sem)

    sums[...] = jnp.zeros_like(sums)
    grid[:, pl.ds(0, 8), :] = jnp.zeros((5, 8, TILE), F32)
    pgrad_rows[:, pl.ds(count, 8), :] = jnp.zeros((CHANS, 8, TILE), F32)
    ext[:, pl.ds(8, TILE), :] = st[...].astype(F32)

    @pl.when(me > 0)
    def _():
        halo_in.wait_recv()
        ext[:, pl.ds(0, 8), :] = halo[...].astype(F32)

    @pl.when(me == 0)
    def _():
        ext[:, pl.ds(0, 8), :] = jnp.zeros((3, 8, ext.shape[2]), F32)

    @pl.when(me < count - 1)
    def _():
        next_in.wait_recv()
        ext[pl.ds(1, 2), pl.ds(8 + TILE, 8), :] = halo_next[...].astype(F32)

    @pl.when(me == count - 1)
    def _():
        ext[pl.ds(1, 2), pl.ds(8 + TILE, 8), :] = jnp.zeros((2, 8, width), F32)

    for i in range(3):
        number = TILE + 8 if i else TILE
        for q in range(width // TILE):
            lanes = pl.ds(q * TILE, TILE)
            total = None
            for j in range(reach + 1):
                term = taps[i, pl.ds(j, 1), lanes] * ext[i, pl.ds(8 - j, number), lanes]
                total = term if total is None else total + term
            local_qkv[i, pl.ds(0, number), lanes] = total

    def slot(index, c):
        if index in (1, 2, 3):
            return index, c
        return (0, 4)[c // 2], c % 2 + (2 if index == 4 else 0)

    def unpack(source, index):
        grid[index, pl.ds(8, count * CHANS), :] = source[...].astype(F32).reshape(count * CHANS, TILE)

    def plane(index, c):
        block, line = slot(index, c)
        return grid[block, pl.ds(8 + line, count, stride=CHANS), :]

    def convolve(index, c):
        here = plane(index, c)
        block, line = slot(index, c)
        before = grid[block, pl.ds(8 - CHANS + line, count, stride=CHANS), :]
        total = own_taps[c, index, pl.ds(0, 1), :] * here
        for j in range(1, reach + 1):
            moved = pltpu.roll(jnp.where(lane >= TILE - j, before, here), j, 1)
            shifts[index, c, j] = moved
            total = total + own_taps[c, index, pl.ds(j, 1), :] * moved
        qkv[index, c] = total
        return total

    size = 2 * TILE
    e1 = dft.at[pl.ds(0, size)]
    e2 = [dft.at[pl.ds((1 + k) * size, size)] for k in range(2)]
    e2t = [dft.at[pl.ds((3 + k) * size, size)] for k in range(2)]
    back = [dft.at[pl.ds(5 * size + k * TILE, TILE)] for k in range(2)]

    def forward(planes, index, h):
        x = jnp.concatenate(planes, 1)
        y = dot(e1[...], jnp.concatenate([x, x], 0))
        re, im = y[:count], y[count:]
        twr, twi = tw[0], tw[1]
        tre, tim = re * twr - im * twi, re * twi + im * twr
        turned = jnp.concatenate(
            [jnp.concatenate([v[:, n * TILE : (n + 1) * TILE] for v in (tre, tim)], 1) for n in range(2)], 0
        )
        high, low = split(turned)
        spec[index, h] = dot(high, e2[0][...]) + dot(low, e2[0][...]) + dot(high, e2[1][...])

    def spectrum(index, h):
        return spec[index, h, :, pl.ds(0, TILE)], spec[index, h, :, pl.ds(TILE, TILE)]

    def inverse(re, im):
        high, low = split(jnp.concatenate([re, im], 1))
        u = dot(high, e2t[0][...]) + dot(low, e2t[0][...]) + dot(high, e2t[1][...])
        ur = jnp.concatenate([u[:count, :TILE], u[count:, :TILE]], 1)
        ui = jnp.concatenate([u[:count, TILE:], u[count:, TILE:]], 1)
        twr, twi = tw[0], tw[1]
        high, low = split(jnp.concatenate([ur * twr + ui * twi, ui * twr - ur * twi], 0))
        return dot(back[0][...], high) + dot(back[1][...], high) + dot(back[0][...], low)

    def put_rows(h, values):
        for n in range(2):
            rows[pl.ds(2 * h + n, count, stride=CHANS), :] = values[:, n * TILE : (n + 1) * TILE]

    def pack(which):
        ret_snd[which] = rows[...].astype(BF16).reshape(count, CHANS, TILE)

    def tap_sums(index, c, grad):
        for j in range(reach + 1):
            moved = plane(index, c) if j == 0 else shifts[index, c, j]
            part = jnp.sum((grad * moved).reshape(count // 8, 8, TILE), 0)
            sums[c * ENTRIES + index * (reach + 1) + j] = part

    others(snd1, rcv1, 0).wait_recv()
    unpack(rcv1.at[:, 0], 1)
    unpack(rcv1.at[:, 1], 2)
    for h in range(2):
        products = [(convolve(1, c) * convolve(2, c)).astype(BF16) for c in (2 * h, 2 * h + 1)]
        forward(products, 0, h)
    others(snd2.at[0], rcv2.at[0], LATER[0]).wait_recv()
    unpack(rcv2.at[0], 3)
    for h in range(2):
        forward([plane(3, c).astype(BF16) for c in (2 * h, 2 * h + 1)], 1, h)
        pr, pi = spectrum(0, h)
        fr, fi = spectrum(1, h)
        put_rows(h, inverse(pr * fr - pi * fi, pr * fi + pi * fr))
    pack(0)
    scatter(ret_snd.at[0], ret_rcv.at[0], 2)

    for c in range(CHANS):
        mixed_rows[c] = rows[pl.ds(c, count, stride=CHANS), :].astype(BF16).astype(F32)
    for h in range(2):
        pair = (2 * h, 2 * h + 1)
        others(snd2.at[1 + h], rcv2.at[1 + h], LATER[1 + h]).wait_recv()
        unpack(rcv2.at[1 + h], (0, 4)[h])
        forward([(plane(4, c) * convolve(0, c)).astype(BF16) for c in pair], 2, h)
        pr, pi = spectrum(0, h)
        fr, fi = spectrum(1, h)
        gr, gi = spectrum(2, h)
        pgrad = inverse(fr * gr + fi * gi, fr * gi - fi * gr)
        put_rows(0, pgrad)
        put_rows(1, inverse(pr * gr + pi * gi, pr * gi - pi * gr) * scale)
        pack(1 + h)
        scatter(ret_snd.at[1 + h], ret_rcv.at[1 + h], 3 + h)
        for n, c in enumerate(pair):
            pgrad_rows[c, pl.ds(0, count), :] = pgrad[:, n * TILE : (n + 1) * TILE].astype(BF16).astype(F32)
    ahead = None
    for c in range(CHANS):
        tap_sums(0, c, plane(4, c) * mixed_rows[c])
        tap_sums(1, c, pgrad_rows[c, pl.ds(0, count), :] * qkv[2, c])
        tap_sums(2, c, pgrad_rows[c, pl.ds(0, count), :] * qkv[1, c])
        place = c * ENTRIES + AHEAD
        moved = pltpu.roll(pgrad_rows[c, pl.ds(1, count), :], place, 1)
        moved = jnp.where((lane >= place) & (lane < place + reach), moved, 0.0)
        ahead = moved if ahead is None else ahead + moved
    entries = jnp.sum(sums[...], 1)
    row = lax.dot_general(
        jnp.ones((8, TILE), F32), entries, (((1,), (1,)), ((), ())),
        precision=lax.Precision.HIGHEST, preferred_element_type=F32,
    )
    small[...] = (row[0:1] * scale + ahead).reshape(count, 1, TILE)
    scatter(small, tall, 5)

    strips = [pl.ds(q * TILE, TILE) for q in range(width // TILE)]

    edge, beyond = cgrad.at[0, pl.ds(0, 8)], cgrad.at[0, pl.ds(TILE, 8)]
    edge_out = remote(edge, beyond, 7, lax.rem(me + count - 1, count))
    edge_in = remote(edge, beyond, 7, me)

    def correlate(streams, first, number):
        for i in streams:
            for lanes in strips:
                total = None
                for j in range(reach + 1):
                    term = taps[i, pl.ds(j, 1), lanes] * cgrad[i, pl.ds(first + j, number), lanes]
                    total = term if total is None else total + term
                sgrad_ref[i, pl.ds(first, number), lanes] = total.astype(BF16)

    @pl.when(me == count - 1)
    def _():
        cgrad[0, pl.ds(TILE, 8), :] = jnp.zeros((8, width), F32)

    others(ret_snd.at[0], ret_rcv.at[0], 2).wait_recv()
    for q, lanes in enumerate(strips):
        mixed = turn_back(ret_rcv.at[0], q)
        gated_ref[:, lanes] = (local_qkv[0, pl.ds(0, TILE), lanes] * mixed).astype(BF16)
        cgrad[0, pl.ds(0, TILE), lanes] = ct[:, lanes].astype(F32) * mixed

    @pl.when(me > 0)
    def _():
        edge_out.start()

    correlate((0,), 0, TILE - 16)
    for h in range(2):
        others(ret_snd.at[1 + h], ret_rcv.at[1 + h], 3 + h).wait_recv()
    for q, lanes in enumerate(strips):
        pgrad = jnp.where(low, turn_back(ret_rcv.at[1], q), pltpu.roll(turn_back(ret_rcv.at[2], q), 2, 1))
        cgrad[1, pl.ds(0, TILE), lanes] = pgrad * local_qkv[2, pl.ds(0, TILE), lanes]
        cgrad[2, pl.ds(0, TILE), lanes] = pgrad * local_qkv[1, pl.ds(0, TILE), lanes]
    for q, lanes in enumerate(strips):
        fgrad = jnp.where(low, pltpu.roll(turn_back(ret_rcv.at[1], q), TILE - 2, 1), turn_back(ret_rcv.at[2], q))
        fgrad_ref[:, lanes] = fgrad.astype(BF16)
    correlate((1, 2), 0, TILE - 16)

    @pl.when(me < count - 1)
    def _():
        edge_in.wait_recv()

    correlate((0,), TILE - 16, 16)
    others(small, tall, 5).wait_recv()
    shared = tall[...].reshape(count, TILE)
    for c in range(CHANS):
        moved = pltpu.roll(shared, TILE - c * ENTRIES, 1) if c else shared
        spread[pl.ds(c, count, stride=CHANS), :] = moved
    terms = reach + 1
    for q, lanes in enumerate(strips):
        by_entry = spread[pl.ds(q * TILE, TILE), :].T
        for i in range(3):
            tgrad_ref[i, :, lanes] = by_entry[i * terms : (i + 1) * terms]
        following = by_entry[AHEAD : AHEAD + 8]
        cgrad[1, pl.ds(TILE, 8), lanes] = following * local_qkv[2, pl.ds(TILE, 8), lanes]
        cgrad[2, pl.ds(TILE, 8), lanes] = following * local_qkv[1, pl.ds(TILE, 8), lanes]
    correlate((1, 2), TILE - 16, 16)
    others(snd1, rcv1, 0).wait_send()
    for k, sem in enumerate(LATER):
        others(snd2.at[k], rcv2.at[k], sem).wait_send()
    for k in range(3):
        others(ret_snd.at[k], ret_rcv.at[k], 2 + k).wait_send()
    others(small, tall, 5).wait_send()

    @pl.when(me < count - 1)
    def _():
        halo_out.wait_send()

    @pl.when(me > 0)
    def _():
        next_out.wait_send()
        edge_out.wait_send()


def result_kernel(*refs):
    number = len(refs) // 2
    sem = refs[-1]
    stores = [
        pltpu.make_async_copy(source, target, sem.at[i])
        for i, (source, target) in enumerate(zip(refs[:number], refs[number : 2 * number]))
    ]
    for store in stores:
        store.start()
    for store in stores:
        store.wait()


def local(streams, taps, filters, cotangent):
    rows, width = filters.shape
    count = lax.axis_size("ctx")
    assert rows == TILE and width == CHANS * count and count == TILE == Y_SIZE * Z_SIZE * X_SIZE
    tables = [jnp.asarray(t) for t in make_tables(count, rows)]
    reach = taps.shape[1] - 1
    hbm = pl.BlockSpec(memory_space=pltpu.HBM)
    vmem = pl.BlockSpec(memory_space=VMEM)
    line = (count, CHANS, TILE)
    pair = (count, 2, CHANS, TILE)
    scratch = [
        VMEM(streams.shape, BF16), VMEM(filters.shape, BF16), VMEM(cotangent.shape, BF16), VMEM(taps.shape, F32),
        *[VMEM(t.shape, t.dtype) for t in tables],
        VMEM(pair, BF16), VMEM((3,) + line, BF16), VMEM(pair, BF16), VMEM((3,) + line, BF16),
        VMEM((CHANS, 3, 8, TILE), F32),
        VMEM((5, 8 + count * CHANS, TILE), F32),
        VMEM((3, CHANS, reach + 1, count, TILE), F32),
        VMEM((3, CHANS, count, TILE), F32),
        VMEM((3, 2, 2 * count, 2 * TILE), F32),
        VMEM((count * CHANS, TILE), F32), VMEM((CHANS, count, TILE), F32), VMEM((CHANS, count + 8, TILE), F32),
        VMEM((3,) + line, BF16), VMEM((3,) + line, BF16),
        VMEM((TILE, 8, TILE), F32), VMEM((count, 1, TILE), F32), VMEM((count, 1, TILE), F32),
        VMEM((count * CHANS, TILE), F32),
        VMEM((3, 8, width), BF16), VMEM((2, 8, width), BF16),
        VMEM((3, 8 + TILE + 8, width), F32),
        VMEM((3, TILE + 8, width), F32),
        VMEM((3, TILE + 8, width), F32),
        pltpu.SemaphoreType.DMA((6,)), pltpu.SemaphoreType.DMA((11,)), pltpu.SemaphoreType.DMA((11,)),
    ]
    parts = pl.pallas_call(
        block_kernel,
        out_shape=[
            jax.ShapeDtypeStruct(cotangent.shape, BF16),
            jax.ShapeDtypeStruct(streams.shape, BF16),
            jax.ShapeDtypeStruct(filters.shape, BF16),
            jax.ShapeDtypeStruct(taps.shape, F32),
        ],
        in_specs=[hbm] * 6,
        out_specs=[vmem] * 4,
        scratch_shapes=scratch,
        compiler_params=pltpu.CompilerParams(
            collective_id=0, has_side_effects=True, vmem_limit_bytes=40 << 20
        ),
    )(*[pltpu.with_memory_space_constraint(x, pltpu.HBM) for x in (streams, filters, cotangent, taps, *tables)])
    return pl.pallas_call(
        result_kernel,
        out_shape=[
            jax.ShapeDtypeStruct(cotangent.shape, BF16),
            jax.ShapeDtypeStruct(streams.shape, BF16),
            jax.ShapeDtypeStruct(filters.shape, BF16),
            jax.ShapeDtypeStruct(taps.shape, F32),
        ],
        in_specs=[vmem] * 4,
        out_specs=[hbm] * 4,
        scratch_shapes=[pltpu.SemaphoreType.DMA((4,))],
        compiler_params=pltpu.CompilerParams(vmem_limit_bytes=8 << 20),
    )(*parts)


def solution(mesh):
    in_specs = (P(None, "ctx", "fft"), P(None, None, "fft"), P("ctx", "fft"), P("ctx", "fft"))
    out_specs = (P("ctx", "fft"), P(None, "ctx", "fft"), P("ctx", "fft"), P(None, None, "fft"))
    return jax.shard_map(local, mesh=mesh, in_specs=in_specs, out_specs=out_specs, check_vma=False)
```

```python
import math

import jax
import jax.numpy as jnp
import numpy as np
from jax import lax
from jax.experimental import pallas as pl
from jax.experimental.pallas import tpu as pltpu
from jax.sharding import PartitionSpec as P

MESH = pl.DeviceIdType.MESH
VMEM = pltpu.VMEM
F32 = jnp.float32
BF16 = jnp.bfloat16
CHANS = 4
TILE = 128
ENTRIES = 32
AHEAD = 24
Y_SIZE, Z_SIZE, X_SIZE = 8, 8, 2
LATER = (1, 8, 10)


def halves(table):
    high = table.astype(BF16)
    return high, (table - high.astype(np.float64)).astype(BF16)


def make_tables(a_size, b_size):
    k1, a, b, k2 = (np.arange(n, dtype=np.int64) for n in (a_size, a_size, b_size, b_size))
    first = (4 * k1[:, None] + 1) * a[None, :] % (4 * a_size) / (4.0 * a_size)
    twist = (4 * k1[:, None] + 1) * b[None, :] % (4 * a_size * b_size) / (4.0 * a_size * b_size)
    second = b[:, None] * k2[None, :] % b_size / float(b_size)
    first, twist, second = (np.exp(-2j * np.pi * x) for x in (first, twist, second))
    e1 = np.concatenate([first.real, first.imag], 0)
    e2 = np.block([[second.real, second.imag], [-second.imag, second.real]])
    back = np.concatenate([first.real.T, first.imag.T], 1) / (a_size * b_size)
    e1 = np.concatenate(halves(e1), 1)
    e2, e2t, back = (np.stack(halves(x)) for x in (e2, e2.T, back))
    twist = np.stack([np.tile(x, (1, 2)) for x in (twist.real, twist.imag)]).astype(np.float32)
    stacked = np.concatenate([x.reshape(-1, 2 * b_size) for x in (e1, e2, e2t, back)], 0)
    return stacked, twist


def dot(a, b):
    return jnp.dot(a, b, preferred_element_type=F32)


def split(x):
    high = x.astype(BF16)
    return high, (x - high.astype(F32)).astype(BF16)


def turn_back(source, q):
    tile = source[pl.ds(q * TILE // CHANS, TILE // CHANS)].astype(F32).reshape(TILE, TILE)
    return tile.T


def block_kernel(
    streams_hbm, filters_hbm, cot_hbm, taps_hbm, dft_hbm, tw_hbm,
    gated_ref, sgrad_ref, fgrad_ref, tgrad_ref,
    st, fl, ct, taps, dft, tw,
    snd1, snd2, rcv1, rcv2, own_taps, grid, shifts, qkv, spec, rows, mixed_rows, pgrad_rows, ret_snd, ret_rcv,
    sums, small, tall, spread, halo, halo_next, ext, local_qkv, cgrad,
    in_sem, send_sem, recv_sem,
):
    count = rcv1.shape[0]
    width = ext.shape[2]
    reach = taps.shape[1] - 1
    scale = 1.0 / math.sqrt(count * TILE)
    me = lax.axis_index("ctx")
    barrier = pltpu.get_barrier_semaphore()

    def remote(source, target, sem, peer):
        return pltpu.make_async_remote_copy(
            source, target, send_sem.at[sem], recv_sem.at[sem], device_id={"ctx": peer}, device_id_type=MESH
        )

    zx_count = Z_SIZE * X_SIZE
    y, zx = me // zx_count, lax.rem(me, zx_count)
    z, x = zx // X_SIZE, lax.rem(zx, X_SIZE)
    planes = [
        lax.rem(z + dz, Z_SIZE) * X_SIZE + lax.rem(x + dx, X_SIZE)
        for dz in (4, 3, 5, 2, 6, 1, 7, 0)
        for dx in (1, 0)
    ]

    def each_peer(visit):
        def row(step, carry):
            half = (step + 1) // 2
            dy = 4 + half - 2 * half * lax.rem(step, 2)
            base = lax.rem(y + dy, Y_SIZE) * zx_count
            for plane_at in planes:
                visit(base + plane_at)
            return carry

        lax.fori_loop(0, Y_SIZE - 1, row, 0)
        for plane_at in planes[:-1]:
            visit(y * zx_count + plane_at)

    loads = [
        pltpu.make_async_copy(source, target, in_sem.at[i])
        for i, (source, target) in enumerate(
            (
                (streams_hbm, st), (filters_hbm, fl), (cot_hbm, ct), (taps_hbm, taps), (dft_hbm, dft),
                (tw_hbm, tw),
            )
        )
    ]
    for load in loads:
        load.start()

    def greet(peer):
        pl.semaphore_signal(barrier, inc=1, device_id={"ctx": peer}, device_id_type=MESH)

    each_peer(greet)

    def turn_out(source, target):
        for q in range(source.shape[1] // TILE):
            tile = source[:, q * TILE : (q + 1) * TILE].astype(F32).T
            target[pl.ds(q * TILE // CHANS, TILE // CHANS)] = tile.astype(BF16).reshape(-1, CHANS, TILE)

    loads[0].wait()
    turn_out(st.at[1], snd1.at[:, 0])
    turn_out(st.at[2], snd1.at[:, 1])
    loads[1].wait()
    turn_out(fl, snd2.at[0])
    loads[2].wait()
    lane = lax.broadcasted_iota(jnp.int32, (TILE, TILE), 1)
    low = lax.rem(lane, CHANS) < 2
    for q in range(width // TILE):
        lanes = pl.ds(q * TILE, TILE)
        place = pl.ds(q * TILE // CHANS, TILE // CHANS)
        first, second = st[0, :, lanes].astype(F32), ct[:, lanes].astype(F32)
        tiles = (
            jnp.where(low, first, pltpu.roll(second, 2, 1)),
            jnp.where(low, pltpu.roll(first, TILE - 2, 1), second),
        )
        for h, tile in enumerate(tiles):
            snd2.at[1 + h][place] = tile.T.astype(BF16).reshape(-1, CHANS, TILE)
    for load in loads[3:]:
        load.wait()
    for i in range(3):
        for c in range(CHANS):
            chosen = lax.broadcasted_iota(jnp.int32, (reach + 1, width), 1) == CHANS * me + c
            tap = jnp.sum(jnp.where(chosen, taps[i], 0.0), 1, keepdims=True)
            own_taps[c, i, pl.ds(0, reach + 1), :] = jnp.broadcast_to(tap, (reach + 1, TILE))

    def scatter(source, target, sem):
        each_peer(lambda peer: remote(source.at[peer], target.at[me], sem, peer).start())
        target[me] = source[me]

    def others(source, target, sem):
        return remote(source.at[pl.ds(0, count - 1)], target.at[pl.ds(0, count - 1)], sem, me)

    pl.semaphore_wait(barrier, count - 1)
    halo_out = remote(st.at[:, pl.ds(TILE - 8, 8)], halo, 6, lax.rem(me + 1, count))
    halo_in = remote(st.at[:, pl.ds(TILE - 8, 8)], halo, 6, me)

    next_out = remote(st.at[pl.ds(1, 2), pl.ds(0, 8)], halo_next, 4 + 5, lax.rem(me + count - 1, count))
    next_in = remote(st.at[pl.ds(1, 2), pl.ds(0, 8)], halo_next, 4 + 5, me)

    scatter(snd1, rcv1, 0)
    for k, sem in enumerate(LATER):
        scatter(snd2.at[k], rcv2.at[k], sem)

    @pl.when(me < count - 1)
    def _():
        halo_out.start()

    @pl.when(me > 0)
    def _():
        next_out.start()

    sums[...] = jnp.zeros_like(sums)
    grid[:, pl.ds(0, 8), :] = jnp.zeros((5, 8, TILE), F32)
    pgrad_rows[:, pl.ds(count, 8), :] = jnp.zeros((CHANS, 8, TILE), F32)

    def slot(index, c):
        if index in (1, 2, 3):
            return index, c
        return (0, 4)[c // 2], c % 2 + (2 if index == 4 else 0)

    def unpack(source, index):
        grid[index, pl.ds(8, count * CHANS), :] = source[...].astype(F32).reshape(count * CHANS, TILE)

    def plane(index, c):
        block, line = slot(index, c)
        return grid[block, pl.ds(8 + line, count, stride=CHANS), :]

    def convolve(index, c):
        here = plane(index, c)
        block, line = slot(index, c)
        before = grid[block, pl.ds(8 - CHANS + line, count, stride=CHANS), :]
        total = own_taps[c, index, pl.ds(0, 1), :] * here
        for j in range(1, reach + 1):
            moved = pltpu.roll(jnp.where(lane >= TILE - j, before, here), j, 1)
            shifts[index, c, j] = moved
            total = total + own_taps[c, index, pl.ds(j, 1), :] * moved
        qkv[index, c] = total
        return total

    size = 2 * TILE
    e1 = dft.at[pl.ds(0, size)]
    e2 = [dft.at[pl.ds((1 + k) * size, size)] for k in range(2)]
    e2t = [dft.at[pl.ds((3 + k) * size, size)] for k in range(2)]
    back = [dft.at[pl.ds(5 * size + k * TILE, TILE)] for k in range(2)]

    def forward(planes, index, h):
        x = jnp.concatenate(planes, 1)
        y = dot(e1[...], jnp.concatenate([x, x], 0))
        re, im = y[:count], y[count:]
        twr, twi = tw[0], tw[1]
        tre, tim = re * twr - im * twi, re * twi + im * twr
        turned = jnp.concatenate(
            [jnp.concatenate([v[:, n * TILE : (n + 1) * TILE] for v in (tre, tim)], 1) for n in range(2)], 0
        )
        high, low = split(turned)
        spec[index, h] = dot(high, e2[0][...]) + dot(low, e2[0][...]) + dot(high, e2[1][...])

    def spectrum(index, h):
        return spec[index, h, :, pl.ds(0, TILE)], spec[index, h, :, pl.ds(TILE, TILE)]

    def inverse(re, im):
        high, low = split(jnp.concatenate([re, im], 1))
        u = dot(high, e2t[0][...]) + dot(low, e2t[0][...]) + dot(high, e2t[1][...])
        ur = jnp.concatenate([u[:count, :TILE], u[count:, :TILE]], 1)
        ui = jnp.concatenate([u[:count, TILE:], u[count:, TILE:]], 1)
        twr, twi = tw[0], tw[1]
        high, low = split(jnp.concatenate([ur * twr + ui * twi, ui * twr - ur * twi], 0))
        return dot(back[0][...], high) + dot(back[1][...], high) + dot(back[0][...], low)

    def put_rows(h, values):
        for n in range(2):
            rows[pl.ds(2 * h + n, count, stride=CHANS), :] = values[:, n * TILE : (n + 1) * TILE]

    def pack(which):
        ret_snd[which] = rows[...].astype(BF16).reshape(count, CHANS, TILE)

    def tap_sums(index, c, grad):
        for j in range(reach + 1):
            moved = plane(index, c) if j == 0 else shifts[index, c, j]
            part = jnp.sum((grad * moved).reshape(count // 8, 8, TILE), 0)
            sums[c * ENTRIES + index * (reach + 1) + j] = part

    others(snd1, rcv1, 0).wait_recv()
    unpack(rcv1.at[:, 0], 1)
    unpack(rcv1.at[:, 1], 2)
    for h in range(2):
        products = [(convolve(1, c) * convolve(2, c)).astype(BF16) for c in (2 * h, 2 * h + 1)]
        forward(products, 0, h)
    others(snd2.at[0], rcv2.at[0], LATER[0]).wait_recv()
    unpack(rcv2.at[0], 3)
    for h in range(2):
        forward([plane(3, c).astype(BF16) for c in (2 * h, 2 * h + 1)], 1, h)
        pr, pi = spectrum(0, h)
        fr, fi = spectrum(1, h)
        put_rows(h, inverse(pr * fr - pi * fi, pr * fi + pi * fr))
    pack(0)
    scatter(ret_snd.at[0], ret_rcv.at[0], 2)

    for c in range(CHANS):
        mixed_rows[c] = rows[pl.ds(c, count, stride=CHANS), :].astype(BF16).astype(F32)
    for h in range(2):
        pair = (2 * h, 2 * h + 1)
        others(snd2.at[1 + h], rcv2.at[1 + h], LATER[1 + h]).wait_recv()
        unpack(rcv2.at[1 + h], (0, 4)[h])
        forward([(plane(4, c) * convolve(0, c)).astype(BF16) for c in pair], 2, h)
        pr, pi = spectrum(0, h)
        fr, fi = spectrum(1, h)
        gr, gi = spectrum(2, h)
        pgrad = inverse(fr * gr + fi * gi, fr * gi - fi * gr)
        put_rows(0, pgrad)
        put_rows(1, inverse(pr * gr + pi * gi, pr * gi - pi * gr) * scale)
        pack(1 + h)
        scatter(ret_snd.at[1 + h], ret_rcv.at[1 + h], 3 + h)
        for n, c in enumerate(pair):
            pgrad_rows[c, pl.ds(0, count), :] = pgrad[:, n * TILE : (n + 1) * TILE].astype(BF16).astype(F32)
    ahead = None
    for c in range(CHANS):
        tap_sums(0, c, plane(4, c) * mixed_rows[c])
        tap_sums(1, c, pgrad_rows[c, pl.ds(0, count), :] * qkv[2, c])
        tap_sums(2, c, pgrad_rows[c, pl.ds(0, count), :] * qkv[1, c])
        place = c * ENTRIES + AHEAD
        moved = pltpu.roll(pgrad_rows[c, pl.ds(1, count), :], place, 1)
        moved = jnp.where((lane >= place) & (lane < place + reach), moved, 0.0)
        ahead = moved if ahead is None else ahead + moved
    entries = jnp.sum(sums[...], 1)
    row = lax.dot_general(
        jnp.ones((8, TILE), F32), entries, (((1,), (1,)), ((), ())),
        precision=lax.Precision.HIGHEST, preferred_element_type=F32,
    )
    small[...] = (row[0:1] * scale + ahead).reshape(count, 1, TILE)
    scatter(small, tall, 5)

    ext[:, pl.ds(8, TILE), :] = st[...].astype(F32)

    @pl.when(me > 0)
    def _():
        halo_in.wait_recv()
        ext[:, pl.ds(0, 8), :] = halo[...].astype(F32)

    @pl.when(me == 0)
    def _():
        ext[:, pl.ds(0, 8), :] = jnp.zeros((3, 8, ext.shape[2]), F32)

    @pl.when(me < count - 1)
    def _():
        next_in.wait_recv()
        ext[pl.ds(1, 2), pl.ds(8 + TILE, 8), :] = halo_next[...].astype(F32)

    @pl.when(me == count - 1)
    def _():
        ext[pl.ds(1, 2), pl.ds(8 + TILE, 8), :] = jnp.zeros((2, 8, width), F32)

    for i in range(3):
        number = TILE + 8 if i else TILE
        for q in range(width // TILE):
            lanes = pl.ds(q * TILE, TILE)
            total = None
            for j in range(reach + 1):
                term = taps[i, pl.ds(j, 1), lanes] * ext[i, pl.ds(8 - j, number), lanes]
                total = term if total is None else total + term
            local_qkv[i, pl.ds(0, number), lanes] = total

    strips = [pl.ds(q * TILE, TILE) for q in range(width // TILE)]

    edge, beyond = cgrad.at[0, pl.ds(0, 8)], cgrad.at[0, pl.ds(TILE, 8)]
    edge_out = remote(edge, beyond, 7, lax.rem(me + count - 1, count))
    edge_in = remote(edge, beyond, 7, me)

    def correlate(streams, first, number):
        for i in streams:
            for lanes in strips:
                total = None
                for j in range(reach + 1):
                    term = taps[i, pl.ds(j, 1), lanes] * cgrad[i, pl.ds(first + j, number), lanes]
                    total = term if total is None else total + term
                sgrad_ref[i, pl.ds(first, number), lanes] = total.astype(BF16)

    @pl.when(me == count - 1)
    def _():
        cgrad[0, pl.ds(TILE, 8), :] = jnp.zeros((8, width), F32)

    others(ret_snd.at[0], ret_rcv.at[0], 2).wait_recv()
    for q, lanes in enumerate(strips):
        mixed = turn_back(ret_rcv.at[0], q)
        gated_ref[:, lanes] = (local_qkv[0, pl.ds(0, TILE), lanes] * mixed).astype(BF16)
        cgrad[0, pl.ds(0, TILE), lanes] = ct[:, lanes].astype(F32) * mixed

    @pl.when(me > 0)
    def _():
        edge_out.start()

    correlate((0,), 0, TILE - 16)
    for h in range(2):
        others(ret_snd.at[1 + h], ret_rcv.at[1 + h], 3 + h).wait_recv()
    for q, lanes in enumerate(strips):
        pgrad = jnp.where(low, turn_back(ret_rcv.at[1], q), pltpu.roll(turn_back(ret_rcv.at[2], q), 2, 1))
        cgrad[1, pl.ds(0, TILE), lanes] = pgrad * local_qkv[2, pl.ds(0, TILE), lanes]
        cgrad[2, pl.ds(0, TILE), lanes] = pgrad * local_qkv[1, pl.ds(0, TILE), lanes]
    for q, lanes in enumerate(strips):
        fgrad = jnp.where(low, pltpu.roll(turn_back(ret_rcv.at[1], q), TILE - 2, 1), turn_back(ret_rcv.at[2], q))
        fgrad_ref[:, lanes] = fgrad.astype(BF16)
    correlate((1, 2), 0, TILE - 16)

    @pl.when(me < count - 1)
    def _():
        edge_in.wait_recv()

    correlate((0,), TILE - 16, 16)
    others(small, tall, 5).wait_recv()
    shared = tall[...].reshape(count, TILE)
    for c in range(CHANS):
        moved = pltpu.roll(shared, TILE - c * ENTRIES, 1) if c else shared
        spread[pl.ds(c, count, stride=CHANS), :] = moved
    terms = reach + 1
    for q, lanes in enumerate(strips):
        by_entry = spread[pl.ds(q * TILE, TILE), :].T
        for i in range(3):
            tgrad_ref[i, :, lanes] = by_entry[i * terms : (i + 1) * terms]
        following = by_entry[AHEAD : AHEAD + 8]
        cgrad[1, pl.ds(TILE, 8), lanes] = following * local_qkv[2, pl.ds(TILE, 8), lanes]
        cgrad[2, pl.ds(TILE, 8), lanes] = following * local_qkv[1, pl.ds(TILE, 8), lanes]
    correlate((1, 2), TILE - 16, 16)
    others(snd1, rcv1, 0).wait_send()
    for k, sem in enumerate(LATER):
        others(snd2.at[k], rcv2.at[k], sem).wait_send()
    for k in range(3):
        others(ret_snd.at[k], ret_rcv.at[k], 2 + k).wait_send()
    others(small, tall, 5).wait_send()

    @pl.when(me < count - 1)
    def _():
        halo_out.wait_send()

    @pl.when(me > 0)
    def _():
        next_out.wait_send()
        edge_out.wait_send()


def result_kernel(*refs):
    number = len(refs) // 2
    sem = refs[-1]
    stores = [
        pltpu.make_async_copy(source, target, sem.at[i])
        for i, (source, target) in enumerate(zip(refs[:number], refs[number : 2 * number]))
    ]
    for store in stores:
        store.start()
    for store in stores:
        store.wait()


def local(streams, taps, filters, cotangent):
    rows, width = filters.shape
    count = lax.axis_size("ctx")
    assert rows == TILE and width == CHANS * count and count == TILE == Y_SIZE * Z_SIZE * X_SIZE
    tables = [jnp.asarray(t) for t in make_tables(count, rows)]
    reach = taps.shape[1] - 1
    hbm = pl.BlockSpec(memory_space=pltpu.HBM)
    vmem = pl.BlockSpec(memory_space=VMEM)
    line = (count, CHANS, TILE)
    pair = (count, 2, CHANS, TILE)
    scratch = [
        VMEM(streams.shape, BF16), VMEM(filters.shape, BF16), VMEM(cotangent.shape, BF16), VMEM(taps.shape, F32),
        *[VMEM(t.shape, t.dtype) for t in tables],
        VMEM(pair, BF16), VMEM((3,) + line, BF16), VMEM(pair, BF16), VMEM((3,) + line, BF16),
        VMEM((CHANS, 3, 8, TILE), F32),
        VMEM((5, 8 + count * CHANS, TILE), F32),
        VMEM((3, CHANS, reach + 1, count, TILE), F32),
        VMEM((3, CHANS, count, TILE), F32),
        VMEM((3, 2, 2 * count, 2 * TILE), F32),
        VMEM((count * CHANS, TILE), F32), VMEM((CHANS, count, TILE), F32), VMEM((CHANS, count + 8, TILE), F32),
        VMEM((3,) + line, BF16), VMEM((3,) + line, BF16),
        VMEM((TILE, 8, TILE), F32), VMEM((count, 1, TILE), F32), VMEM((count, 1, TILE), F32),
        VMEM((count * CHANS, TILE), F32),
        VMEM((3, 8, width), BF16), VMEM((2, 8, width), BF16),
        VMEM((3, 8 + TILE + 8, width), F32),
        VMEM((3, TILE + 8, width), F32),
        VMEM((3, TILE + 8, width), F32),
        pltpu.SemaphoreType.DMA((6,)), pltpu.SemaphoreType.DMA((11,)), pltpu.SemaphoreType.DMA((11,)),
    ]
    parts = pl.pallas_call(
        block_kernel,
        out_shape=[
            jax.ShapeDtypeStruct(cotangent.shape, BF16),
            jax.ShapeDtypeStruct(streams.shape, BF16),
            jax.ShapeDtypeStruct(filters.shape, BF16),
            jax.ShapeDtypeStruct(taps.shape, F32),
        ],
        in_specs=[hbm] * 6,
        out_specs=[vmem] * 4,
        scratch_shapes=scratch,
        compiler_params=pltpu.CompilerParams(
            collective_id=0, has_side_effects=True, vmem_limit_bytes=40 << 20
        ),
    )(*[pltpu.with_memory_space_constraint(x, pltpu.HBM) for x in (streams, filters, cotangent, taps, *tables)])
    return pl.pallas_call(
        result_kernel,
        out_shape=[
            jax.ShapeDtypeStruct(cotangent.shape, BF16),
            jax.ShapeDtypeStruct(streams.shape, BF16),
            jax.ShapeDtypeStruct(filters.shape, BF16),
            jax.ShapeDtypeStruct(taps.shape, F32),
        ],
        in_specs=[vmem] * 4,
        out_specs=[hbm] * 4,
        scratch_shapes=[pltpu.SemaphoreType.DMA((4,))],
        compiler_params=pltpu.CompilerParams(vmem_limit_bytes=8 << 20),
    )(*parts)


def solution(mesh):
    in_specs = (P(None, "ctx", "fft"), P(None, None, "fft"), P("ctx", "fft"), P("ctx", "fft"))
    out_specs = (P("ctx", "fft"), P(None, "ctx", "fft"), P("ctx", "fft"), P(None, None, "fft"))
    return jax.shard_map(local, mesh=mesh, in_specs=in_specs, out_specs=out_specs, check_vma=False)
```
